128 devices in a mesh: samp: 32 (over y, z, core), layer: 4 (over x).
Axes of the slice: x: 4, y: 4, z: 4, core: 2. Of those that a mesh axis runs over, the one named last changes fastest.
Arguments:
- spins: int32 [256, 256], P('samp'), may hold values 0 or 1
- activations: bfloat16 [256, 8, 256, 256], P('samp', 'layer'), may hold values from -6 to 6
- cotangents: bfloat16 [256, 8, 256, 256], P('samp', 'layer'), may hold values from -0.023925781 to 0.023925781
- offdiag: float32 [256], P('samp'), may hold values from -24 to 24
Outputs:
- weights: float32 [256], P('samp')
- update: float32 [8, 256, 256], P('layer', 'samp')
The draws below stay inside these ranges and needn't reach their ends.
All inputs are finite; a program needn't handle non-finite values. No bound on the sum of `spins` on one device may be relied on, other than what follows from the above.
Results may differ from the reference program's by a relative error of at most 0.0029.
Values may be sent and summed in bfloat16 or wider, within the bound.
A program may use at most 64 MiB of HBM per device.

```python
import jax
import jax.numpy as jnp
from jax import lax

SIDE = 16
SITES = 256
D = 256
MATS = 8
SAMPLES = 256


def plant(values, rng, smallest, top_value):
    longest = values.shape.index(max(values.shape))
    spots = []
    for shift in (0, 1):
        where = [jax.random.randint(jax.random.fold_in(rng, axis), (), 0, length) for axis, length in enumerate(values.shape)]
        where[longest] = (where[longest] + shift) % values.shape[longest]
        spots.append(tuple(where))
    return values.at[spots[0]].set(smallest).at[spots[1]].set(top_value)


def block_scale(stream_key, shape, split, smallest, top_value):
    level = 1.0
    for position, shards_of in split:
        heights = jax.random.uniform(jax.random.fold_in(jax.random.fold_in(stream_key, 6), position), (shards_of,), jnp.float32, smallest / len(split), top_value / len(split))
        level = level * jnp.repeat(jnp.exp(heights), shape[position] // shards_of).reshape((-1,) + (1,) * (len(shape) - 1 - position))
    return level


def bell_draw(own_key, shape, spread, most, cuts=(), kind=jnp.bfloat16):
    array = jax.random.normal(own_key, shape, jnp.float32) * spread
    if len(cuts) > 0:
        array = block_scale(own_key, shape, cuts, -0.22, 0.18) * array
    return jnp.clip(array, min=-most, max=most).astype(kind)


def setup_inputs(seed: int = 0) -> dict:
    seeds = jax.random.split(jax.random.key(seed), 5)
    spins = plant((jax.random.randint(seeds[0], (SAMPLES, SITES), 0, 2) < 1).astype(jnp.int32), jax.random.fold_in(seeds[0], 1), 0, 1)
    activations = bell_draw(seeds[1], (SAMPLES, MATS, SITES, D), 1.0, 6.0, ((0, 32), (1, 4)))
    cotangents = bell_draw(seeds[2], (SAMPLES, MATS, SITES, D), 0.004, 0.023925781, ((0, 32), (1, 4)))
    offdiag = bell_draw(seeds[3], (SAMPLES,), 4.0, 24.0, ((0, 32),), jnp.float32)
    return {"spins": spins, "activations": activations, "cotangents": cotangents, "offdiag": offdiag}


shift_ratio = 0.1

def local_energy(spins, offdiag):
    zvals = (2 * spins - 1).astype(jnp.float32).reshape(spins.shape[0], SIDE, SIDE)
    bonds = zvals * jnp.roll(zvals, -1, 2) + zvals * jnp.roll(zvals, -1, 1)
    return offdiag + lax.optimization_barrier(jnp.sum(bonds, axis=(1, 2)))

def jacobian_rows(act_mat, cot_mat):
    jac = jnp.einsum('sad,sae->sde', act_mat.astype(jnp.float32), cot_mat.astype(jnp.float32)).astype(jnp.bfloat16)
    flat = jac.reshape(jac.shape[0], -1).astype(jnp.float32)
    return flat - lax.optimization_barrier(jnp.mean(flat, axis=0, keepdims=True))

def reference(spins, activations, cotangents, offdiag):
    energy = local_energy(spins, offdiag)
    total = energy.shape[0]
    eps = (energy - jnp.mean(energy)) / jnp.sqrt(jnp.float32(total))
    act_t = jnp.swapaxes(activations, 0, 1)
    cot_t = jnp.swapaxes(cotangents, 0, 1)

    def add_gram(carry, pair):
        centered = jacobian_rows(pair[0], pair[1])
        return (carry + jnp.dot(centered, centered.T, precision=lax.Precision.HIGHEST), None)
    gram, _ = lax.scan(add_gram, jnp.zeros((total, total), jnp.float32), (act_t, cot_t))
    gram = gram / total
    shift = shift_ratio * jnp.trace(gram) / total
    chol = jnp.linalg.cholesky(gram + shift * jnp.eye(total, dtype=jnp.float32))
    half = jax.scipy.linalg.solve_triangular(chol, eps, lower=True)
    weights = jax.scipy.linalg.solve_triangular(chol.T, half, lower=False)

    def project(pair):
        centered = jacobian_rows(pair[0], pair[1])
        return jnp.dot(weights, centered, precision=lax.Precision.HIGHEST).reshape(D, D)
    update = lax.map(project, (act_t, cot_t))
    return (weights, update)
```

```python
import functools

import jax
import jax.numpy as jnp
from jax import lax
from jax.experimental import pallas as pl
from jax.experimental.pallas import tpu as pltpu
from jax.sharding import PartitionSpec as P

SIDE = 16


shift_ratio = 0.1
highest = lax.Precision.HIGHEST


def laid_out(parts, dim):
    parts = jnp.moveaxis(parts, 0, dim)
    dims = parts.shape
    return parts.reshape(*dims[:dim], dims[dim] * dims[dim + 1], *dims[dim + 2 :])


def copy_for_each(shard, axis):
    length = lax.axis_size(axis)
    return lax.all_to_all(
        jnp.broadcast_to(shard[None], (length, *shard.shape)), axis, 0, 0, tiled=True
    )


def gather_directly(shard, axis, dim):
    return laid_out(copy_for_each(shard, axis), dim)


def local_energy(spins, offdiag):
    zvals = (2 * spins - 1).astype(jnp.float32).reshape(spins.shape[0], SIDE, SIDE)
    bonds = zvals * jnp.roll(zvals, -1, 2) + zvals * jnp.roll(zvals, -1, 1)
    return offdiag + jnp.sum(bonds, axis=(1, 2))


def tile_inverse(tile):
    order = tile.shape[0]
    sub = lax.broadcasted_iota(jnp.int32, (order, order), 0)
    lane = lax.broadcasted_iota(jnp.int32, (order, order), 1)
    sub_col = lax.broadcasted_iota(jnp.int32, (order, 1), 0)
    lane_row = lax.broadcasted_iota(jnp.int32, (1, order), 1)
    for k in range(order):
        row = tile[k : k + 1, :]
        col = tile[:, k : k + 1]
        inv_pivot = 1.0 / tile[k : k + 1, k : k + 1]
        scaled = jnp.where(lane_row == k, 1.0, row) * inv_pivot
        kept = jnp.where((lane == k) | (sub == k), 0.0, tile)
        tile = kept - jnp.where(sub_col == k, -1.0, col) * scaled
    return tile


def solve_kernel(block, gram_ref, rhs_ref, out_ref, work):
    order = gram_ref.shape[0]
    work[0:order, :] = gram_ref[...]
    work[order : order + 8, :] = jnp.broadcast_to(rhs_ref[...], (8, order))
    lane = lax.broadcasted_iota(jnp.int32, (1, order), 1)
    for k in range(order // block):
        own = slice(k * block, (k + 1) * block)
        below = slice((k + 1) * block, order + 8)
        inverse = tile_inverse(work[own, own])
        scaled = jnp.dot(work[below, own], inverse, precision=highest, preferred_element_type=jnp.float32)
        inside = (lane >= k * block) & (lane < (k + 1) * block)
        pivot_rows = jnp.where(inside, 0.0, work[own, :])
        work[below, :] = work[below, :] - jnp.dot(
            scaled, pivot_rows, precision=highest, preferred_element_type=jnp.float32
        )
        work[below, own] = scaled
    out_ref[...] = work[order : order + 1, :]


def solve(matrix, rhs):
    order = matrix.shape[0]
    return pl.pallas_call(
        functools.partial(solve_kernel, 64),
        out_shape=jax.ShapeDtypeStruct((1, order), jnp.float32),
        in_specs=[pl.BlockSpec(memory_space=pltpu.VMEM)] * 2,
        out_specs=pl.BlockSpec(memory_space=pltpu.VMEM),
        scratch_shapes=[pltpu.VMEM((order + 8, order), jnp.float32)],
    )(matrix, rhs[None, :])[0]


def sum_directly(partial_sum, axes):
    devices = 1
    for axis in axes:
        devices = devices * lax.axis_size(axis)
    rows = partial_sum.shape[0] // devices
    pieces = lax.all_to_all(
        partial_sum.reshape(devices, rows, -1), axes, 0, 0, tiled=True
    )
    own = jnp.sum(pieces, axis=0)
    spread = lax.all_to_all(
        jnp.broadcast_to(own[None], pieces.shape), axes, 0, 0, tiled=True
    )
    return spread.reshape(partial_sum.shape)


def body(spins, activations, cotangents, offdiag):
    s_local = spins.shape[0]
    energy_local = local_energy(spins, offdiag)
    energy = gather_directly(energy_local, "samp", 0)
    total = energy.shape[0]
    eps = (energy - jnp.mean(energy)) / jnp.sqrt(jnp.float32(total))
    jac = jnp.einsum(
        "ksad,ksae->ksde", activations, cotangents, preferred_element_type=jnp.float32
    ).astype(jnp.bfloat16)
    regrouped = lax.all_to_all(jac, "samp", split_axis=2, concat_axis=0, tiled=True)
    flat = regrouped.reshape(total, -1)
    col_mean = jnp.mean(flat, axis=0, dtype=jnp.float32)
    raw_gram = jnp.dot(flat, flat.T, preferred_element_type=jnp.float32)
    row_dots = jnp.dot(flat.astype(jnp.float32), col_mean, precision=highest)
    mean_square = jnp.sum(col_mean * col_mean)
    partial_value = (raw_gram - row_dots[:, None] - row_dots[None, :] + mean_square) / total
    gram = sum_directly(partial_value, ("samp", "layer"))
    shift = shift_ratio * jnp.trace(gram) / total
    weights = solve(gram + shift * jnp.eye(total, dtype=jnp.float32), eps)
    start = lax.axis_index("samp") * s_local
    own_weights = lax.dynamic_slice_in_dim(weights, start, s_local)
    coeffs_all = weights - jnp.mean(weights)
    update = jnp.dot(coeffs_all, flat.astype(jnp.float32), precision=highest).reshape(
        regrouped.shape[1:]
    )
    return (own_weights, update)


def solution(mesh):
    placed = (
        P("samp", None),
        P("samp", "layer", None, None),
        P("samp", "layer", None, None),
        P("samp"),
    )
    return jax.shard_map(
        body,
        mesh=mesh,
        in_specs=placed,
        out_specs=(P("samp"), P("layer", "samp", None)),
        check_vma=False,
    )
```

```python
import functools

import jax
import jax.numpy as jnp
from jax import lax
from jax.experimental import pallas as pl
from jax.experimental.pallas import tpu as pltpu
from jax.sharding import PartitionSpec as P

SIDE = 16
SHIFT_RATIO = 0.1
highest = lax.Precision.HIGHEST
MESH = pl.DeviceIdType.MESH
f32 = jnp.float32


def iota(shape, dim):
    return lax.broadcasted_iota(jnp.int32, shape, dim)


def local_energy(spins, offdiag_row):
    samples, sites = spins.shape
    z = (2 * spins - 1).astype(f32)
    column = iota((samples, sites), 1) % SIDE
    next_column = jnp.where(
        column == SIDE - 1,
        pltpu.roll(z, SIDE - 1, 1),
        pltpu.roll(z, sites - 1, 1),
    )
    next_row = pltpu.roll(z, sites - SIDE, 1)
    bonds = jnp.sum(z * (next_column + next_row), axis=1, keepdims=True)
    square = jnp.broadcast_to(offdiag_row, (samples, samples))
    diagonal = iota((samples, samples), 0) == iota((samples, samples), 1)
    return bonds + jnp.sum(jnp.where(diagonal, square, 0.0), axis=1, keepdims=True)


def gram_kernel(
    peers, layers,
    spins_ref, offdiag_ref, act_hbm, cot_hbm,
    rows_ref, gram_ref,
    act, cot, wide, outgoing, own_gram, pieces, sums, spread,
    in_sem, own_sem, row_send, row_recv, piece_send, piece_recv,
    sum_send, sum_recv, spread_send, spread_recv,
):
    samples, mats, sites, width = act.shape
    share = width // peers
    me = lax.axis_index("samp")
    layer = lax.axis_index("layer")

    def loads(s):
        return (
            pltpu.make_async_copy(act_hbm.at[s], act.at[s], in_sem.at[0, s]),
            pltpu.make_async_copy(cot_hbm.at[s], cot.at[s], in_sem.at[1, s]),
        )

    for s in range(samples):
        for load in loads(s):
            load.start()

    barrier = pltpu.get_barrier_semaphore()

    def greet(i, carry):
        pl.semaphore_signal(
            barrier, inc=1, device_id={"samp": lax.rem(me + i, peers)}, device_id_type=MESH
        )
        return carry

    lax.fori_loop(1, peers, greet, 0)
    for i in range(1, layers):
        pl.semaphore_signal(
            barrier, inc=1, device_id={"layer": lax.rem(layer + i, layers)}, device_id_type=MESH
        )

    energy = local_energy(spins_ref[...], offdiag_ref[...])

    def row_copy(m, peer):
        return pltpu.make_async_remote_copy(
            src_ref=outgoing.at[m, peer],
            dst_ref=rows_ref.at[m, :, me],
            send_sem=row_send.at[m],
            recv_sem=row_recv.at[m],
            device_id={"samp": peer},
            device_id_type=MESH,
        )

    for m in range(mats):
        for s in range(samples):
            if m == 0:
                for load in loads(s):
                    load.wait()
            jac = lax.dot_general(
                act[s, m], cot[s, m], (((0,), (0,)), ((), ())), preferred_element_type=f32
            )
            for h in range(width // 128):
                wide[pl.ds(h * width * samples + s, width, stride=samples), :] = jac[:, h * 128 : (h + 1) * 128]
        for h in range(width // 128):
            for k in range(peers):
                start = h * width * samples + k * share * samples
                block = wide[start : start + share * samples, :]
                outgoing[m, k, :, :, h * 128 : (h + 1) * 128] = block.reshape(share, samples, 128).astype(jnp.bfloat16)
        if m == 0:
            pl.semaphore_wait(barrier, peers + layers - 2)

        def send(i, carry):
            row_copy(m, lax.rem(me + i, peers)).start()
            return carry

        lax.fori_loop(1, peers, send, 0)
        pltpu.make_async_copy(outgoing.at[m, me], rows_ref.at[m, :, me], own_sem.at[m]).start()

    for m in range(mats):
        pltpu.make_async_copy(outgoing.at[m, me], rows_ref.at[m, :, me], own_sem.at[m]).wait()
        many = rows_ref.at[m, :, 0 : peers - 1]
        pltpu.make_async_copy(many, many, row_recv.at[m]).wait()
        total = None
        for r in range(share):
            rows = rows_ref[m, r].reshape(peers * samples, width)
            term = lax.dot_general(
                rows, rows, (((1,), (1,)), ((), ())), preferred_element_type=f32
            )
            total = term if total is None else total + term
        if m == 0:
            own_gram[...] = total
        else:
            own_gram[...] = own_gram[...] + total

    def piece_copy(peer):
        return pltpu.make_async_remote_copy(
            src_ref=own_gram.at[pl.ds(pl.multiple_of(peer * samples, samples), samples)],
            dst_ref=pieces.at[me],
            send_sem=piece_send,
            recv_sem=piece_recv,
            device_id={"samp": peer},
            device_id_type=MESH,
        )

    def send_piece(i, carry):
        piece_copy(lax.rem(me + i, peers)).start()
        return carry

    lax.fori_loop(1, peers, send_piece, 0)
    pieces[me] = own_gram[pl.ds(pl.multiple_of(me * samples, samples), samples)]
    many = pieces.at[0 : peers - 1]
    pltpu.make_async_copy(many, many, piece_recv).wait()
    sums[layer] = jnp.sum(pieces[...], axis=0)

    def sum_copy(i):
        return pltpu.make_async_remote_copy(
            src_ref=sums.at[layer],
            dst_ref=sums.at[layer],
            send_sem=sum_send.at[i],
            recv_sem=sum_recv.at[i],
            device_id={"layer": lax.rem(layer + i, layers)},
            device_id_type=MESH,
        )

    for i in range(1, layers):
        sum_copy(i).start()
    for i in range(1, layers):
        sum_copy(i).wait_recv()
    spread[:, 0:256] = jnp.sum(sums[...], axis=0)
    spread[:, 256:384] = jnp.broadcast_to(energy, (samples, 128))

    mine = pl.ds(pl.multiple_of(me * samples, samples), samples)

    def spread_copy(peer):
        return pltpu.make_async_remote_copy(
            src_ref=spread,
            dst_ref=gram_ref.at[mine],
            send_sem=spread_send,
            recv_sem=spread_recv,
            device_id={"samp": peer},
            device_id_type=MESH,
        )

    def send_spread(i, carry):
        spread_copy(lax.rem(me + i, peers)).start()
        return carry

    lax.fori_loop(1, peers, send_spread, 0)
    gram_ref[mine] = spread[...]
    for m in range(mats):
        many = outgoing.at[m, 0 : peers - 1]
        pltpu.make_async_copy(many, many, row_send.at[m]).wait()
    many = own_gram.at[0 : (peers - 1) * samples]
    pltpu.make_async_copy(many, many, piece_send).wait()
    for i in range(1, layers):
        sum_copy(i).wait_send()
    many = gram_ref.at[0 : (peers - 1) * samples]
    pltpu.make_async_copy(many, many, spread_recv).wait()
    pltpu.make_async_copy(many, many, spread_send).wait()


def gram_and_rows(spins, activations, cotangents, offdiag):
    samples, mats, sites, width = activations.shape
    peers, layers = lax.axis_size("samp"), lax.axis_size("layer")
    total, share = peers * samples, width // peers
    bf16 = jnp.bfloat16
    vmem = pl.BlockSpec(memory_space=pltpu.VMEM)
    dma = pltpu.SemaphoreType.DMA
    return pl.pallas_call(
        functools.partial(gram_kernel, peers, layers),
        out_shape=(
            jax.ShapeDtypeStruct((mats, share, peers, samples, width), bf16),
            jax.ShapeDtypeStruct((total, total + 128), f32),
        ),
        in_specs=[vmem, vmem, pl.BlockSpec(memory_space=pl.ANY), pl.BlockSpec(memory_space=pl.ANY)],
        out_specs=(vmem, vmem),
        scratch_shapes=[
            pltpu.VMEM(activations.shape, bf16),
            pltpu.VMEM(cotangents.shape, bf16),
            pltpu.VMEM((width // 128 * width * samples, 128), f32),
            pltpu.VMEM((mats, peers, share, samples, width), bf16),
            pltpu.VMEM((total, total), f32),
            pltpu.VMEM((peers, samples, total), f32),
            pltpu.VMEM((layers, samples, total), f32),
            pltpu.VMEM((samples, total + 128), f32),
            dma((2, samples)),
            dma((mats,)),
            dma((mats,)),
            dma((mats,)),
            dma,
            dma,
            dma((layers,)),
            dma((layers,)),
            dma,
            dma,
        ],
        compiler_params=pltpu.CompilerParams(
            collective_id=0, has_side_effects=True, vmem_limit_bytes=48 << 20
        ),
    )(spins, offdiag[None, :], activations, cotangents)


def tile_inverse(tile):
    order = tile.shape[0]
    sub, lane = iota((order, order), 0), iota((order, order), 1)
    sub_col, lane_row = iota((order, 1), 0), iota((1, order), 1)
    for k in range(order):
        row = tile[k : k + 1, :]
        col = tile[:, k : k + 1]
        inv_pivot = 1.0 / tile[k : k + 1, k : k + 1]
        scaled = jnp.where(lane_row == k, 1.0, row) * inv_pivot
        kept = jnp.where((lane == k) | (sub == k), 0.0, tile)
        tile = kept - jnp.where(sub_col == k, -1.0, col) * scaled
    return tile


def solve_kernel(block, rows_ref, gram_ref, weights_ref, update_ref, work):
    mats, share, peers, samples, width = rows_ref.shape
    total = peers * samples
    me = lax.axis_index("samp")
    raw = gram_ref[:, 0:total]
    means = jnp.mean(raw, axis=1, keepdims=True)
    diagonal = iota((total, total), 0) == iota((total, total), 1)

    def as_row(col):
        return jnp.sum(jnp.where(diagonal, col, 0.0), axis=0, keepdims=True)

    means_row = as_row(means)
    gram = (raw - means - means_row + jnp.mean(means_row)) / total
    trace = jnp.sum(jnp.where(diagonal, gram, 0.0))
    work[0:total, :] = gram + jnp.where(diagonal, SHIFT_RATIO * trace / total, 0.0)
    energy = as_row(gram_ref[:, total : total + 1])
    eps = (energy - jnp.mean(energy)) / jnp.sqrt(f32(total))
    work[total : total + 8, :] = jnp.broadcast_to(eps, (8, total))
    lane = iota((1, total), 1)
    for k in range(total // block):
        own = slice(k * block, (k + 1) * block)
        below = slice((k + 1) * block, total + 8)
        inverse = tile_inverse(work[own, own])
        scaled = jnp.dot(work[below, own], inverse, precision=highest, preferred_element_type=f32)
        inside = (lane >= k * block) & (lane < (k + 1) * block)
        pivot_rows = jnp.where(inside, 0.0, work[own, :])
        work[below, :] = work[below, :] - jnp.dot(
            scaled, pivot_rows, precision=highest, preferred_element_type=f32
        )
        work[below, own] = scaled
    weights = work[total : total + 1, :]
    weights_ref[...] = pltpu.roll(weights, total - me * samples, 1)[:, 0:samples]
    coeffs = weights - jnp.mean(weights)
    first = coeffs.astype(jnp.bfloat16)
    rest = coeffs - first.astype(f32)
    second = rest.astype(jnp.bfloat16)
    third = (rest - second.astype(f32)).astype(jnp.bfloat16)
    split = jnp.concatenate(
        [first.astype(f32), second.astype(f32), third.astype(f32), jnp.zeros((5, total), f32)], axis=0
    ).astype(jnp.bfloat16)
    for m in range(mats):
        for r in range(share):
            rows = rows_ref[m, r].reshape(total, width)
            parts = jnp.dot(split, rows, preferred_element_type=f32)
            update_ref[m, r : r + 1, :] = jnp.sum(parts, axis=0, keepdims=True)


def solve_and_update(rows, gram):
    mats, share, peers, samples, width = rows.shape
    total = peers * samples
    vmem = pl.BlockSpec(memory_space=pltpu.VMEM)
    return pl.pallas_call(
        functools.partial(solve_kernel, 64),
        out_shape=(
            jax.ShapeDtypeStruct((1, samples), f32),
            jax.ShapeDtypeStruct((mats, share, width), f32),
        ),
        in_specs=[vmem, vmem],
        out_specs=(vmem, vmem),
        scratch_shapes=[pltpu.VMEM((total + 8, total), f32)],
    )(rows, gram)


def body(spins, activations, cotangents, offdiag):
    rows, gram = gram_and_rows(spins, activations, cotangents, offdiag)
    weights, update = solve_and_update(rows, gram)
    return weights[0], update


def solution(mesh):
    placed = (
        P("samp", None),
        P("samp", "layer", None, None),
        P("samp", "layer", None, None),
        P("samp"),
    )
    return jax.shard_map(
        body,
        mesh=mesh,
        in_specs=placed,
        out_specs=(P("samp"), P("layer", "samp", None)),
        check_vma=False,
    )
```

```python
import functools

import jax
import jax.numpy as jnp
from jax import lax
from jax.experimental import pallas as pl
from jax.experimental.pallas import tpu as pltpu
from jax.sharding import PartitionSpec as P

SIDE = 16
SHIFT_RATIO = 0.1
highest = lax.Precision.HIGHEST
MESH = pl.DeviceIdType.MESH
f32 = jnp.float32
CHIPS = (2, 2), (2, 1), (1, 2), (2, 3), (3, 2), (1, 1), (3, 3), (1, 3), (3, 1), (2, 0), (0, 2), (1, 0), (3, 0), (0, 1), (0, 3)
FAR_FIRST = [(y, z, c) for c in (0, 1) for y, z in CHIPS] + [(0, 0, 1)]


def peer_at(me, step):
    y, z, core = step
    row, col = me // 8, me // 2 % 4
    return (row + y) % 4 * 8 + (col + z) % 4 * 2 + (me + core) % 2


def iota(shape, dim):
    return lax.broadcasted_iota(jnp.int32, shape, dim)


def local_energy(spins, offdiag_row):
    samples, sites = spins.shape
    z = (2 * spins - 1).astype(f32)
    column = iota((samples, sites), 1) % SIDE
    next_column = jnp.where(
        column == SIDE - 1,
        pltpu.roll(z, SIDE - 1, 1),
        pltpu.roll(z, sites - 1, 1),
    )
    next_row = pltpu.roll(z, sites - SIDE, 1)
    bonds = jnp.sum(z * (next_column + next_row), axis=1, keepdims=True)
    square = jnp.broadcast_to(offdiag_row, (samples, samples))
    diagonal = iota((samples, samples), 0) == iota((samples, samples), 1)
    energy = bonds + jnp.sum(jnp.where(diagonal, square, 0.0), axis=1, keepdims=True)
    repeated = iota((samples, sites), 1) % samples == iota((samples, sites), 0)
    return jnp.sum(jnp.where(repeated, energy, 0.0), axis=0, keepdims=True)


def gram_kernel(
    peers, layers,
    spins_hbm, offdiag_hbm, act_hbm, cot_hbm,
    rows_ref, gram_ref, energy_ref,
    spins, offdiag, act, cot, wide, outgoing, own_gram, pieces, sums, spread, energy,
    small_sem, energy_send, energy_recv,
    in_sem, own_sem, row_send, row_recv, piece_send, piece_recv,
    sum_send, sum_recv, spread_send, spread_recv,
):
    samples, mats, sites, width = act.shape
    share = width // peers
    me = lax.axis_index("samp")
    layer = lax.axis_index("layer")

    def loads(s):
        return (
            pltpu.make_async_copy(act_hbm.at[s], act.at[s], in_sem.at[0, s]),
            pltpu.make_async_copy(cot_hbm.at[s], cot.at[s], in_sem.at[1, s]),
        )

    small = (
        pltpu.make_async_copy(spins_hbm, spins, small_sem.at[0]),
        pltpu.make_async_copy(offdiag_hbm, offdiag, small_sem.at[1]),
    )
    for load in small:
        load.start()
    for s in range(samples):
        for load in loads(s):
            load.start()

    barrier = pltpu.get_barrier_semaphore()

    def greet(i, carry):
        pl.semaphore_signal(
            barrier, inc=1, device_id={"samp": lax.rem(me + i, peers)}, device_id_type=MESH
        )
        return carry

    lax.fori_loop(1, peers, greet, 0)
    for i in range(1, layers):
        pl.semaphore_signal(
            barrier, inc=1, device_id={"layer": lax.rem(layer + i, layers)}, device_id_type=MESH
        )

    for load in small:
        load.wait()
    energy[...] = local_energy(spins[...], offdiag[...])
    steps = [peer_at(me, step) for step in FAR_FIRST]

    def energy_copy(peer):
        return pltpu.make_async_remote_copy(
            src_ref=energy,
            dst_ref=energy_ref.at[me],
            send_sem=energy_send,
            recv_sem=energy_recv,
            device_id={"samp": peer},
            device_id_type=MESH,
        )

    def row_copy(m, peer):
        return pltpu.make_async_remote_copy(
            src_ref=outgoing.at[m, peer],
            dst_ref=rows_ref.at[m, :, me],
            send_sem=row_send.at[m],
            recv_sem=row_recv.at[m],
            device_id={"samp": peer},
            device_id_type=MESH,
        )

    for m in range(mats):
        for s in range(samples):
            if m == 0:
                for load in loads(s):
                    load.wait()
            jac = lax.dot_general(
                act[s, m], cot[s, m], (((0,), (0,)), ((), ())), preferred_element_type=f32
            )
            for h in range(width // 128):
                wide[pl.ds(h * width * samples + s, width, stride=samples), :] = jac[:, h * 128 : (h + 1) * 128]
        for h in range(width // 128):
            for k in range(peers):
                start = h * width * samples + k * share * samples
                block = wide[start : start + share * samples, :]
                outgoing[m, k, :, :, h * 128 : (h + 1) * 128] = block.reshape(share, samples, 128).astype(jnp.bfloat16)
        if m == 0:
            pl.semaphore_wait(barrier, peers + layers - 2)
        for peer in steps:
            row_copy(m, peer).start()
        if m == 0:
            for peer in steps:
                energy_copy(peer).start()
            energy_ref[me] = energy[...]
        pltpu.make_async_copy(outgoing.at[m, me], rows_ref.at[m, :, me], own_sem.at[m]).start()

    for m in range(mats):
        pltpu.make_async_copy(outgoing.at[m, me], rows_ref.at[m, :, me], own_sem.at[m]).wait()
        many = rows_ref.at[m, :, 0 : peers - 1]
        pltpu.make_async_copy(many, many, row_recv.at[m]).wait()
        total = None
        for r in range(share):
            rows = rows_ref[m, r].reshape(peers * samples, width)
            term = lax.dot_general(
                rows, rows, (((1,), (1,)), ((), ())), preferred_element_type=f32
            )
            total = term if total is None else total + term
        if m == 0:
            own_gram[...] = total
        else:
            own_gram[...] = own_gram[...] + total

    def piece_copy(peer):
        return pltpu.make_async_remote_copy(
            src_ref=own_gram.at[pl.ds(pl.multiple_of(peer * samples, samples), samples)],
            dst_ref=pieces.at[me],
            send_sem=piece_send,
            recv_sem=piece_recv,
            device_id={"samp": peer},
            device_id_type=MESH,
        )

    for peer in steps:
        piece_copy(peer).start()
    pieces[me] = own_gram[pl.ds(pl.multiple_of(me * samples, samples), samples)]
    many = pieces.at[0 : peers - 1]
    pltpu.make_async_copy(many, many, piece_recv).wait()
    sums[layer] = jnp.sum(pieces[...], axis=0)

    def sum_copy(i):
        return pltpu.make_async_remote_copy(
            src_ref=sums.at[layer],
            dst_ref=sums.at[layer],
            send_sem=sum_send.at[i],
            recv_sem=sum_recv.at[i],
            device_id={"layer": lax.rem(layer + i, layers)},
            device_id_type=MESH,
        )

    for i in (2, 1, 3):
        sum_copy(i).start()
    for i in range(1, layers):
        sum_copy(i).wait_recv()
    spread[...] = jnp.sum(sums[...], axis=0)

    mine = pl.ds(pl.multiple_of(me * samples, samples), samples)

    def spread_copy(peer):
        return pltpu.make_async_remote_copy(
            src_ref=spread,
            dst_ref=gram_ref.at[mine],
            send_sem=spread_send,
            recv_sem=spread_recv,
            device_id={"samp": peer},
            device_id_type=MESH,
        )

    for peer in steps:
        spread_copy(peer).start()
    gram_ref[mine] = spread[...]
    for m in range(mats):
        many = outgoing.at[m, 0 : peers - 1]
        pltpu.make_async_copy(many, many, row_send.at[m]).wait()
    many = energy_ref.at[0 : peers - 1]
    pltpu.make_async_copy(many, many, energy_send).wait()
    pltpu.make_async_copy(many, many, energy_recv).wait()
    many = own_gram.at[0 : (peers - 1) * samples]
    pltpu.make_async_copy(many, many, piece_send).wait()
    for i in range(1, layers):
        sum_copy(i).wait_send()
    many = gram_ref.at[0 : (peers - 1) * samples]
    pltpu.make_async_copy(many, many, spread_recv).wait()
    pltpu.make_async_copy(many, many, spread_send).wait()


def gram_and_rows(spins, activations, cotangents, offdiag):
    samples, mats, sites, width = activations.shape
    peers, layers = lax.axis_size("samp"), lax.axis_size("layer")
    total, share = peers * samples, width // peers
    bf16 = jnp.bfloat16
    vmem = pl.BlockSpec(memory_space=pltpu.VMEM)
    dma = pltpu.SemaphoreType.DMA
    return pl.pallas_call(
        functools.partial(gram_kernel, peers, layers),
        out_shape=(
            jax.ShapeDtypeStruct((mats, share, peers, samples, width), bf16),
            jax.ShapeDtypeStruct((total, total), f32),
            jax.ShapeDtypeStruct((peers, 1, total), f32),
        ),
        in_specs=[pl.BlockSpec(memory_space=pltpu.HBM)] * 4,
        out_specs=(vmem, vmem, vmem),
        scratch_shapes=[
            pltpu.VMEM(spins.shape, jnp.int32),
            pltpu.VMEM((1, samples), f32),
            pltpu.VMEM(activations.shape, bf16),
            pltpu.VMEM(cotangents.shape, bf16),
            pltpu.VMEM((width // 128 * width * samples, 128), f32),
            pltpu.VMEM((mats, peers, share, samples, width), bf16),
            pltpu.VMEM((total, total), f32),
            pltpu.VMEM((peers, samples, total), f32),
            pltpu.VMEM((layers, samples, total), f32),
            pltpu.VMEM((samples, total), f32),
            pltpu.VMEM((1, total), f32),
            dma((2,)),
            dma,
            dma,
            dma((2, samples)),
            dma((mats,)),
            dma((mats,)),
            dma((mats,)),
            dma,
            dma,
            dma((layers,)),
            dma((layers,)),
            dma,
            dma,
        ],
        compiler_params=pltpu.CompilerParams(
            collective_id=0, has_side_effects=True, vmem_limit_bytes=20 << 20
        ),
    )(*(pltpu.with_memory_space_constraint(a, pltpu.HBM) for a in (spins, offdiag[None, :], activations, cotangents)))


def tile_inverse(tile):
    order = tile.shape[0]
    sub, lane = iota((order, order), 0), iota((order, order), 1)
    sub_col, lane_row = iota((order, 1), 0), iota((1, order), 1)
    for k in range(order):
        row = tile[k : k + 1, :]
        col = tile[:, k : k + 1]
        inv_pivot = 1.0 / tile[k : k + 1, k : k + 1]
        scaled = jnp.where(lane_row == k, 1.0, row) * inv_pivot
        kept = jnp.where((lane == k) | (sub == k), 0.0, tile)
        tile = kept - jnp.where(sub_col == k, -1.0, col) * scaled
    return tile


def solve_kernel(block, rows_ref, gram_ref, energy_ref, weights_ref, update_ref, work):
    mats, share, peers, samples, width = rows_ref.shape
    total = peers * samples
    me = lax.axis_index("samp")
    raw = gram_ref[...]
    means = jnp.mean(raw, axis=1, keepdims=True)
    diagonal = iota((total, total), 0) == iota((total, total), 1)

    def as_row(col):
        return jnp.sum(jnp.where(diagonal, col, 0.0), axis=0, keepdims=True)

    means_row = as_row(means)
    gram = (raw - means - means_row + jnp.mean(means_row)) / total
    trace = jnp.sum(jnp.where(diagonal, gram, 0.0))
    work[0:total, :] = gram + jnp.where(diagonal, SHIFT_RATIO * trace / total, 0.0)
    every = energy_ref[...].reshape(peers, total)
    held = iota((peers, total), 1) // samples == iota((peers, total), 0)
    energy = jnp.sum(jnp.where(held, every, 0.0), axis=0, keepdims=True)
    eps = (energy - jnp.mean(energy)) / jnp.sqrt(f32(total))
    work[total : total + 8, :] = jnp.broadcast_to(eps, (8, total))
    lane = iota((1, total), 1)
    for k in range(total // block):
        own = slice(k * block, (k + 1) * block)
        below = slice((k + 1) * block, total + 8)
        inverse = tile_inverse(work[own, own])
        scaled = jnp.dot(work[below, own], inverse, precision=highest, preferred_element_type=f32)
        inside = (lane >= k * block) & (lane < (k + 1) * block)
        pivot_rows = jnp.where(inside, 0.0, work[own, :])
        work[below, :] = work[below, :] - jnp.dot(
            scaled, pivot_rows, precision=highest, preferred_element_type=f32
        )
        work[below, own] = scaled
    weights = work[total : total + 1, :]
    weights_ref[...] = pltpu.roll(weights, total - me * samples, 1)[:, 0:samples]
    coeffs = weights - jnp.mean(weights)
    first = coeffs.astype(jnp.bfloat16)
    rest = coeffs - first.astype(f32)
    second = rest.astype(jnp.bfloat16)
    third = (rest - second.astype(f32)).astype(jnp.bfloat16)
    split = jnp.concatenate(
        [first.astype(f32), second.astype(f32), third.astype(f32), jnp.zeros((5, total), f32)], axis=0
    ).astype(jnp.bfloat16)
    for m in range(mats):
        for r in range(share):
            rows = rows_ref[m, r].reshape(total, width)
            parts = jnp.dot(split, rows, preferred_element_type=f32)
            update_ref[m, r : r + 1, :] = jnp.sum(parts, axis=0, keepdims=True)


def solve_and_update(rows, gram, energy):
    mats, share, peers, samples, width = rows.shape
    total = peers * samples
    vmem = pl.BlockSpec(memory_space=pltpu.VMEM)
    return pl.pallas_call(
        functools.partial(solve_kernel, 64),
        out_shape=(
            jax.ShapeDtypeStruct((1, samples), f32),
            jax.ShapeDtypeStruct((mats, share, width), f32),
        ),
        in_specs=[vmem, vmem, vmem],
        out_specs=(vmem, vmem),
        scratch_shapes=[pltpu.VMEM((total + 8, total), f32)],
        compiler_params=pltpu.CompilerParams(vmem_limit_bytes=20 << 20),
    )(rows, gram, energy)


def body(spins, activations, cotangents, offdiag):
    rows, gram, energy = gram_and_rows(spins, activations, cotangents, offdiag)
    weights, update = solve_and_update(rows, gram, energy)
    return weights[0], update


def solution(mesh):
    placed = (
        P("samp", None),
        P("samp", "layer", None, None),
        P("samp", "layer", None, None),
        P("samp"),
    )
    return jax.shard_map(
        body,
        mesh=mesh,
        in_specs=placed,
        out_specs=(P("samp"), P("layer", "samp", None)),
        check_vma=False,
    )
```

```python
import functools

import jax
import jax.numpy as jnp
from jax import lax
from jax.experimental import pallas as pl
from jax.experimental.pallas import tpu as pltpu
from jax.sharding import PartitionSpec as P

SIDE = 16
SHIFT_RATIO = 0.1
highest = lax.Precision.HIGHEST
MESH = pl.DeviceIdType.MESH
f32 = jnp.float32
CHIPS = (2, 2), (2, 1), (1, 2), (2, 3), (3, 2), (1, 1), (3, 3), (1, 3), (3, 1), (2, 0), (0, 2), (1, 0), (3, 0), (0, 1), (0, 3)
FAR_FIRST = [(y, z, c) for c in (0, 1) for y, z in CHIPS] + [(0, 0, 1)]


def peer_at(me, step):
    y, z, core = step
    row, col = me // 8, me // 2 % 4
    return (row + y) % 4 * 8 + (col + z) % 4 * 2 + (me + core) % 2


def iota(shape, dim):
    return lax.broadcasted_iota(jnp.int32, shape, dim)


def local_energy(spins, offdiag_row):
    samples, sites = spins.shape
    z = (2 * spins - 1).astype(f32)
    column = iota((samples, sites), 1) % SIDE
    next_column = jnp.where(
        column == SIDE - 1,
        pltpu.roll(z, SIDE - 1, 1),
        pltpu.roll(z, sites - 1, 1),
    )
    next_row = pltpu.roll(z, sites - SIDE, 1)
    bonds = jnp.sum(z * (next_column + next_row), axis=1, keepdims=True)
    square = jnp.broadcast_to(offdiag_row, (samples, samples))
    diagonal = iota((samples, samples), 0) == iota((samples, samples), 1)
    energy = bonds + jnp.sum(jnp.where(diagonal, square, 0.0), axis=1, keepdims=True)
    repeated = iota((samples, sites), 1) % samples == iota((samples, sites), 0)
    return jnp.sum(jnp.where(repeated, energy, 0.0), axis=0, keepdims=True)


def gram_kernel(
    peers, layers,
    spins_hbm, offdiag_hbm, act_hbm, cot_hbm,
    rows_ref, gram_ref, energy_ref,
    spins, offdiag, act, cot, wide, outgoing, own_gram, pieces, sums, spread, energy,
    small_sem, energy_send, energy_recv,
    in_sem, own_sem, row_send, row_recv, piece_send, piece_recv,
    sum_send, sum_recv, spread_send, spread_recv,
):
    samples, mats, sites, width = act.shape
    share = width // peers
    me = lax.axis_index("samp")
    layer = lax.axis_index("layer")

    def loads(s):
        return (
            pltpu.make_async_copy(act_hbm.at[s], act.at[s], in_sem.at[0, s]),
            pltpu.make_async_copy(cot_hbm.at[s], cot.at[s], in_sem.at[1, s]),
        )

    small = (
        pltpu.make_async_copy(spins_hbm, spins, small_sem.at[0]),
        pltpu.make_async_copy(offdiag_hbm, offdiag, small_sem.at[1]),
    )
    for load in small:
        load.start()
    for s in range(samples):
        for load in loads(s):
            load.start()

    barrier = pltpu.get_barrier_semaphore()

    def greet(i, carry):
        pl.semaphore_signal(
            barrier, inc=1, device_id={"samp": lax.rem(me + i, peers)}, device_id_type=MESH
        )
        return carry

    lax.fori_loop(1, peers, greet, 0)
    for i in range(1, layers):
        pl.semaphore_signal(
            barrier, inc=1, device_id={"layer": lax.rem(layer + i, layers)}, device_id_type=MESH
        )

    for load in small:
        load.wait()
    energy[...] = local_energy(spins[...], offdiag[...])
    steps = [peer_at(me, step) for step in FAR_FIRST]

    def energy_copy(peer):
        return pltpu.make_async_remote_copy(
            src_ref=energy,
            dst_ref=energy_ref.at[me],
            send_sem=energy_send,
            recv_sem=energy_recv,
            device_id={"samp": peer},
            device_id_type=MESH,
        )

    def row_copy(m, peer):
        return pltpu.make_async_remote_copy(
            src_ref=outgoing.at[m, peer],
            dst_ref=rows_ref.at[m, :, me],
            send_sem=row_send.at[m],
            recv_sem=row_recv.at[m],
            device_id={"samp": peer},
            device_id_type=MESH,
        )

    for m in range(mats):
        for s in range(samples):
            if m == 0:
                for load in loads(s):
                    load.wait()
            jac = lax.dot_general(
                act[s, m], cot[s, m], (((0,), (0,)), ((), ())), preferred_element_type=f32
            )
            for h in range(width // 128):
                wide[pl.ds(h * width * samples + s, width, stride=samples), :] = jac[:, h * 128 : (h + 1) * 128]
        for h in range(width // 128):
            for k in range(peers):
                start = h * width * samples + k * share * samples
                block = wide[start : start + share * samples, :]
                outgoing[m, k, :, :, h * 128 : (h + 1) * 128] = block.reshape(share, samples, 128).astype(jnp.bfloat16)
        if m == 0:
            pl.semaphore_wait(barrier, peers + layers - 2)
        for peer in steps:
            row_copy(m, peer).start()
        if m == 0:
            for peer in steps:
                energy_copy(peer).start()
            energy_ref[me] = energy[...]
        pltpu.make_async_copy(outgoing.at[m, me], rows_ref.at[m, :, me], own_sem.at[m]).start()

    for m in range(mats):
        pltpu.make_async_copy(outgoing.at[m, me], rows_ref.at[m, :, me], own_sem.at[m]).wait()
        many = rows_ref.at[m, :, 0 : peers - 1]
        pltpu.make_async_copy(many, many, row_recv.at[m]).wait()
        total = None
        for r in range(share):
            rows = rows_ref[m, r].reshape(peers * samples, width)
            term = lax.dot_general(
                rows, rows, (((1,), (1,)), ((), ())), preferred_element_type=f32
            )
            total = term if total is None else total + term
        if m == 0:
            own_gram[...] = total
        else:
            own_gram[...] = own_gram[...] + total

    def piece_copy(peer):
        return pltpu.make_async_remote_copy(
            src_ref=own_gram.at[pl.ds(pl.multiple_of(peer * samples, samples), samples)],
            dst_ref=pieces.at[me],
            send_sem=piece_send,
            recv_sem=piece_recv,
            device_id={"samp": peer},
            device_id_type=MESH,
        )

    for peer in steps:
        piece_copy(peer).start()
    pieces[me] = own_gram[pl.ds(pl.multiple_of(me * samples, samples), samples)]
    many = pieces.at[0 : peers - 1]
    pltpu.make_async_copy(many, many, piece_recv).wait()
    sums[layer] = jnp.sum(pieces[...], axis=0)

    def sum_copy(i):
        return pltpu.make_async_remote_copy(
            src_ref=sums.at[layer],
            dst_ref=sums.at[layer],
            send_sem=sum_send.at[i],
            recv_sem=sum_recv.at[i],
            device_id={"layer": lax.rem(layer + i, layers)},
            device_id_type=MESH,
        )

    for i in (2, 1, 3):
        sum_copy(i).start()
    for i in range(1, layers):
        sum_copy(i).wait_recv()
    spread[...] = jnp.sum(sums[...], axis=0)

    mine = pl.ds(pl.multiple_of(me * samples, samples), samples)

    def spread_copy(peer):
        return pltpu.make_async_remote_copy(
            src_ref=spread,
            dst_ref=gram_ref.at[mine],
            send_sem=spread_send,
            recv_sem=spread_recv,
            device_id={"samp": peer},
            device_id_type=MESH,
        )

    for peer in steps:
        spread_copy(peer).start()
    gram_ref[mine] = spread[...]
    for m in range(mats):
        many = outgoing.at[m, 0 : peers - 1]
        pltpu.make_async_copy(many, many, row_send.at[m]).wait()
    many = energy_ref.at[0 : peers - 1]
    pltpu.make_async_copy(many, many, energy_send).wait()
    pltpu.make_async_copy(many, many, energy_recv).wait()
    many = own_gram.at[0 : (peers - 1) * samples]
    pltpu.make_async_copy(many, many, piece_send).wait()
    for i in range(1, layers):
        sum_copy(i).wait_send()
    many = gram_ref.at[0 : (peers - 1) * samples]
    pltpu.make_async_copy(many, many, spread_recv).wait()
    pltpu.make_async_copy(many, many, spread_send).wait()


def gram_and_rows(spins, activations, cotangents, offdiag):
    samples, mats, sites, width = activations.shape
    peers, layers = lax.axis_size("samp"), lax.axis_size("layer")
    total, share = peers * samples, width // peers
    bf16 = jnp.bfloat16
    vmem = pl.BlockSpec(memory_space=pltpu.VMEM)
    dma = pltpu.SemaphoreType.DMA
    return pl.pallas_call(
        functools.partial(gram_kernel, peers, layers),
        out_shape=(
            jax.ShapeDtypeStruct((mats, share, peers, samples, width), bf16),
            jax.ShapeDtypeStruct((total, total), f32),
            jax.ShapeDtypeStruct((peers, 1, total), f32),
        ),
        in_specs=[pl.BlockSpec(memory_space=pltpu.HBM)] * 4,
        out_specs=(vmem, vmem, vmem),
        scratch_shapes=[
            pltpu.VMEM(spins.shape, jnp.int32),
            pltpu.VMEM((1, samples), f32),
            pltpu.VMEM(activations.shape, bf16),
            pltpu.VMEM(cotangents.shape, bf16),
            pltpu.VMEM((width // 128 * width * samples, 128), f32),
            pltpu.VMEM((mats, peers, share, samples, width), bf16),
            pltpu.VMEM((total, total), f32),
            pltpu.VMEM((peers, samples, total), f32),
            pltpu.VMEM((layers, samples, total), f32),
            pltpu.VMEM((samples, total), f32),
            pltpu.VMEM((1, total), f32),
            dma((2,)),
            dma,
            dma,
            dma((2, samples)),
            dma((mats,)),
            dma((mats,)),
            dma((mats,)),
            dma,
            dma,
            dma((layers,)),
            dma((layers,)),
            dma,
            dma,
        ],
        compiler_params=pltpu.CompilerParams(
            collective_id=0, has_side_effects=True, vmem_limit_bytes=20 << 20
        ),
    )(*(pltpu.with_memory_space_constraint(a, pltpu.HBM) for a in (spins, offdiag[None, :], activations, cotangents)))


def minus_inverse(entry, order):
    at = lambda i, j: entry[min(i, j), max(i, j)]
    for p in range(0, order, 2):
        q = p + 1
        first, cross, second = entry[p, p], entry[p, q], entry[q, q]
        scale = 1.0 / (first * second - cross * cross)
        inv_pp, inv_pq, inv_qq = second * scale, cross * scale, first * scale
        others = [i for i in range(order) if i not in (p, q)]
        gain = {
            i: (
                at(i, p) * inv_pp - at(i, q) * inv_pq,
                at(i, q) * inv_qq - at(i, p) * inv_pq,
            )
            for i in others
        }
        fresh = {}
        for x, i in enumerate(others):
            for j in others[x:]:
                fresh[i, j] = entry[i, j] - (gain[i][0] * at(j, p) + gain[i][1] * at(j, q))
            fresh[min(i, p), max(i, p)] = gain[i][0]
            fresh[min(i, q), max(i, q)] = gain[i][1]
        fresh[p, p], fresh[p, q], fresh[q, q] = -inv_pp, inv_pq, -inv_qq
        entry = fresh
        at = lambda i, j, entry=entry: entry[min(i, j), max(i, j)]
    return entry


def tree_sum(terms):
    while len(terms) > 1:
        terms = [a + b for a, b in zip(terms[::2], terms[1::2], strict=True)]
    return terms[0]


def sweep(groups, k):
    shape = groups[k].shape
    lane, sub = iota(shape, 1), iota(shape, 0)
    start = 8 * k
    pivot_rows = [jnp.broadcast_to(groups[k][i : i + 1, :], shape) for i in range(8)]
    entry = {
        (i, j): jnp.broadcast_to(pivot_rows[i][:, start + j : start + j + 1], shape)
        for i in range(8)
        for j in range(i, 8)
    }
    entry = minus_inverse(entry, 8)
    inside = (lane >= start) & (lane < start + 8)
    marked = [
        jnp.where(inside, jnp.where(lane == start + j, -1.0, 0.0), pivot_rows[j]) for j in range(8)
    ]
    scaled = [
        tree_sum([entry[min(i, j), max(i, j)] * marked[j] for j in range(8)]) for i in range(8)
    ]
    swept = []
    for v, group in enumerate(groups):
        if v == k:
            fresh = -scaled[7]
            for i in range(7):
                fresh = jnp.where(sub == i, -scaled[i], fresh)
        else:
            fresh = jnp.where(inside, 0.0, group) + tree_sum(
                [jnp.broadcast_to(group[:, start + i : start + i + 1], shape) * scaled[i] for i in range(8)]
            )
        swept.append(fresh)
    return swept


def solve(matrix, inverse, rhs):
    half = matrix.shape[0] // 2
    dot = functools.partial(jnp.dot, precision=highest, preferred_element_type=f32)
    count = half // 8
    groups = [matrix[8 * v : 8 * v + 8, 0:half] for v in range(count)]
    groups.append(jnp.broadcast_to(rhs[:, 0:half], (8, half)))
    for k in range(count):
        groups = sweep(groups, k)
    for v in range(count):
        inverse[8 * v : 8 * v + 8, :] = groups[v]
    top = groups[count]
    cross = -dot(matrix[half : 2 * half, 0:half], inverse[...])
    rest = matrix[half : 2 * half, half : 2 * half] - dot(cross, matrix[0:half, half : 2 * half])
    groups = [rest[8 * v : 8 * v + 8, :] for v in range(count)]
    groups.append(rhs[:, half : 2 * half] - dot(top, matrix[0:half, half : 2 * half]))
    for k in range(count):
        groups = sweep(groups, k)
    bottom = groups[count]
    top = top - dot(bottom, cross)
    return jnp.concatenate([top[0:1, :], bottom[0:1, :]], axis=1)


def solve_kernel(rows_ref, gram_ref, energy_ref, weights_ref, update_ref, work, inverse):
    mats, share, peers, samples, width = rows_ref.shape
    total = peers * samples
    me = lax.axis_index("samp")
    raw = gram_ref[...]
    means = jnp.mean(raw, axis=1, keepdims=True)
    diagonal = iota((total, total), 0) == iota((total, total), 1)

    def as_row(col):
        return jnp.sum(jnp.where(diagonal, col, 0.0), axis=0, keepdims=True)

    means_row = as_row(means)
    gram = (raw - means - means_row + jnp.mean(means_row)) / total
    trace = jnp.sum(jnp.where(diagonal, gram, 0.0))
    work[...] = gram + jnp.where(diagonal, SHIFT_RATIO * trace / total, 0.0)
    every = energy_ref[...].reshape(peers, total)
    held = iota((peers, total), 1) // samples == iota((peers, total), 0)
    energy = jnp.sum(jnp.where(held, every, 0.0), axis=0, keepdims=True)
    eps = (energy - jnp.mean(energy)) / jnp.sqrt(f32(total))
    weights = solve(work, inverse, eps)
    weights_ref[...] = pltpu.roll(weights, total - me * samples, 1)[:, 0:samples]
    coeffs = weights - jnp.mean(weights)
    first = coeffs.astype(jnp.bfloat16)
    rest = coeffs - first.astype(f32)
    second = rest.astype(jnp.bfloat16)
    third = (rest - second.astype(f32)).astype(jnp.bfloat16)
    split = jnp.concatenate(
        [first.astype(f32), second.astype(f32), third.astype(f32), jnp.zeros((5, total), f32)], axis=0
    ).astype(jnp.bfloat16)
    for m in range(mats):
        for r in range(share):
            rows = rows_ref[m, r].reshape(total, width)
            parts = jnp.dot(split, rows, preferred_element_type=f32)
            update_ref[m, r : r + 1, :] = jnp.sum(parts, axis=0, keepdims=True)


def solve_and_update(rows, gram, energy):
    mats, share, peers, samples, width = rows.shape
    total = peers * samples
    vmem = pl.BlockSpec(memory_space=pltpu.VMEM)
    return pl.pallas_call(
        solve_kernel,
        out_shape=(
            jax.ShapeDtypeStruct((1, samples), f32),
            jax.ShapeDtypeStruct((mats, share, width), f32),
        ),
        in_specs=[vmem, vmem, vmem],
        out_specs=(vmem, vmem),
        scratch_shapes=[pltpu.VMEM((total, total), f32), pltpu.VMEM((total // 2, total // 2), f32)],
        compiler_params=pltpu.CompilerParams(vmem_limit_bytes=20 << 20),
    )(rows, gram, energy)


def body(spins, activations, cotangents, offdiag):
    rows, gram, energy = gram_and_rows(spins, activations, cotangents, offdiag)
    weights, update = solve_and_update(rows, gram, energy)
    return weights[0], update


def solution(mesh):
    placed = (
        P("samp", None),
        P("samp", "layer", None, None),
        P("samp", "layer", None, None),
        P("samp"),
    )
    return jax.shard_map(
        body,
        mesh=mesh,
        in_specs=placed,
        out_specs=(P("samp"), P("layer", "samp", None)),
        check_vma=False,
    )
```

```python
import functools

import jax
import jax.numpy as jnp
from jax import lax
from jax.experimental import pallas as pl
from jax.experimental.pallas import tpu as pltpu
from jax.sharding import PartitionSpec as P

SIDE = 16
SHIFT_RATIO = 0.1
highest = lax.Precision.HIGHEST
MESH = pl.DeviceIdType.MESH
f32 = jnp.float32
CHIPS = (2, 2), (2, 1), (1, 2), (2, 3), (3, 2), (1, 1), (3, 3), (1, 3), (3, 1), (2, 0), (0, 2), (1, 0), (3, 0), (0, 1), (0, 3)
FAR_FIRST = [(y, z, c) for c in (0, 1) for y, z in CHIPS] + [(0, 0, 1)]


def peer_at(me, step):
    y, z, core = step
    row, col = me // 8, me // 2 % 4
    return (row + y) % 4 * 8 + (col + z) % 4 * 2 + (me + core) % 2


def iota(shape, dim):
    return lax.broadcasted_iota(jnp.int32, shape, dim)


def local_energy(spins, offdiag_row):
    samples, sites = spins.shape
    z = (2 * spins - 1).astype(f32)
    column = iota((samples, sites), 1) % SIDE
    next_column = jnp.where(
        column == SIDE - 1,
        pltpu.roll(z, SIDE - 1, 1),
        pltpu.roll(z, sites - 1, 1),
    )
    next_row = pltpu.roll(z, sites - SIDE, 1)
    bonds = jnp.sum(z * (next_column + next_row), axis=1, keepdims=True)
    square = jnp.broadcast_to(offdiag_row, (samples, samples))
    diagonal = iota((samples, samples), 0) == iota((samples, samples), 1)
    energy = bonds + jnp.sum(jnp.where(diagonal, square, 0.0), axis=1, keepdims=True)
    repeated = iota((samples, sites), 1) % samples == iota((samples, sites), 0)
    return jnp.sum(jnp.where(repeated, energy, 0.0), axis=0, keepdims=True)


def gram_kernel(
    peers, layers,
    spins_hbm, offdiag_hbm, act_hbm, cot_hbm,
    rows_ref, gram_ref, energy_ref,
    spins, offdiag, act, cot, wide, outgoing, own_gram, pieces, sums, spread, energy,
    small_sem, energy_send, energy_recv,
    in_sem, own_sem, row_send, row_recv, piece_send, piece_recv,
    sum_send, sum_recv, spread_send, spread_recv,
):
    samples, mats, sites, width = act.shape
    share = width // peers
    me = lax.axis_index("samp")
    layer = lax.axis_index("layer")

    def loads(s):
        return (
            pltpu.make_async_copy(act_hbm.at[s], act.at[s], in_sem.at[0, s]),
            pltpu.make_async_copy(cot_hbm.at[s], cot.at[s], in_sem.at[1, s]),
        )

    small = (
        pltpu.make_async_copy(spins_hbm, spins, small_sem.at[0]),
        pltpu.make_async_copy(offdiag_hbm, offdiag, small_sem.at[1]),
    )
    for load in small:
        load.start()
    for s in range(samples):
        for load in loads(s):
            load.start()

    barrier = pltpu.get_barrier_semaphore()

    def greet(i, carry):
        pl.semaphore_signal(
            barrier, inc=1, device_id={"samp": lax.rem(me + i, peers)}, device_id_type=MESH
        )
        return carry

    lax.fori_loop(1, peers, greet, 0)
    for i in range(1, layers):
        pl.semaphore_signal(
            barrier, inc=1, device_id={"layer": lax.rem(layer + i, layers)}, device_id_type=MESH
        )

    for load in small:
        load.wait()
    energy[...] = local_energy(spins[...], offdiag[...])
    steps = [peer_at(me, step) for step in FAR_FIRST]

    def energy_copy(peer):
        return pltpu.make_async_remote_copy(
            src_ref=energy,
            dst_ref=energy_ref.at[me],
            send_sem=energy_send,
            recv_sem=energy_recv,
            device_id={"samp": peer},
            device_id_type=MESH,
        )

    def row_copy(m, peer):
        return pltpu.make_async_remote_copy(
            src_ref=outgoing.at[m, peer],
            dst_ref=rows_ref.at[m, :, me],
            send_sem=row_send.at[m],
            recv_sem=row_recv.at[m],
            device_id={"samp": peer},
            device_id_type=MESH,
        )

    for m in range(mats):
        for s in range(samples):
            if m == 0:
                for load in loads(s):
                    load.wait()
            jac = lax.dot_general(
                act[s, m], cot[s, m], (((0,), (0,)), ((), ())), preferred_element_type=f32
            )
            for h in range(width // 128):
                wide[pl.ds(h * width * samples + s, width, stride=samples), :] = jac[:, h * 128 : (h + 1) * 128]
        for h in range(width // 128):
            for k in range(peers):
                start = h * width * samples + k * share * samples
                block = wide[start : start + share * samples, :]
                outgoing[m, k, :, :, h * 128 : (h + 1) * 128] = block.reshape(share, samples, 128).astype(jnp.bfloat16)
        if m == 0:
            pl.semaphore_wait(barrier, peers + layers - 2)
        for peer in steps:
            row_copy(m, peer).start()
        if m == 0:
            for peer in steps:
                energy_copy(peer).start()
            energy_ref[me] = energy[...]
        pltpu.make_async_copy(outgoing.at[m, me], rows_ref.at[m, :, me], own_sem.at[m]).start()

    for m in range(mats):
        pltpu.make_async_copy(outgoing.at[m, me], rows_ref.at[m, :, me], own_sem.at[m]).wait()
        many = rows_ref.at[m, :, 0 : peers - 1]
        pltpu.make_async_copy(many, many, row_recv.at[m]).wait()
        total = None
        for r in range(share):
            rows = rows_ref[m, r].reshape(peers * samples, width)
            term = lax.dot_general(
                rows, rows, (((1,), (1,)), ((), ())), preferred_element_type=f32
            )
            total = term if total is None else total + term
        if m == 0:
            own_gram[...] = total
        else:
            own_gram[...] = own_gram[...] + total

    def piece_copy(peer):
        return pltpu.make_async_remote_copy(
            src_ref=own_gram.at[pl.ds(pl.multiple_of(peer * samples, samples), samples)],
            dst_ref=pieces.at[me],
            send_sem=piece_send,
            recv_sem=piece_recv,
            device_id={"samp": peer},
            device_id_type=MESH,
        )

    for peer in steps:
        piece_copy(peer).start()
    pieces[me] = own_gram[pl.ds(pl.multiple_of(me * samples, samples), samples)]
    many = pieces.at[0 : peers - 1]
    pltpu.make_async_copy(many, many, piece_recv).wait()
    sums[layer] = jnp.sum(pieces[...], axis=0)

    def sum_copy(i):
        return pltpu.make_async_remote_copy(
            src_ref=sums.at[layer],
            dst_ref=sums.at[layer],
            send_sem=sum_send.at[i],
            recv_sem=sum_recv.at[i],
            device_id={"layer": lax.rem(layer + i, layers)},
            device_id_type=MESH,
        )

    for i in (2, 1, 3):
        sum_copy(i).start()
    for i in range(1, layers):
        sum_copy(i).wait_recv()
    spread[...] = jnp.sum(sums[...], axis=0)

    mine = pl.ds(pl.multiple_of(me * samples, samples), samples)

    def spread_copy(peer):
        return pltpu.make_async_remote_copy(
            src_ref=spread,
            dst_ref=gram_ref.at[mine],
            send_sem=spread_send,
            recv_sem=spread_recv,
            device_id={"samp": peer},
            device_id_type=MESH,
        )

    for peer in steps:
        spread_copy(peer).start()
    gram_ref[mine] = spread[...]
    for m in range(mats):
        many = outgoing.at[m, 0 : peers - 1]
        pltpu.make_async_copy(many, many, row_send.at[m]).wait()
    many = energy_ref.at[0 : peers - 1]
    pltpu.make_async_copy(many, many, energy_send).wait()
    pltpu.make_async_copy(many, many, energy_recv).wait()
    many = own_gram.at[0 : (peers - 1) * samples]
    pltpu.make_async_copy(many, many, piece_send).wait()
    for i in range(1, layers):
        sum_copy(i).wait_send()
    many = gram_ref.at[0 : (peers - 1) * samples]
    pltpu.make_async_copy(many, many, spread_recv).wait()
    pltpu.make_async_copy(many, many, spread_send).wait()


def gram_and_rows(spins, activations, cotangents, offdiag):
    samples, mats, sites, width = activations.shape
    peers, layers = lax.axis_size("samp"), lax.axis_size("layer")
    total, share = peers * samples, width // peers
    bf16 = jnp.bfloat16
    vmem = pl.BlockSpec(memory_space=pltpu.VMEM)
    dma = pltpu.SemaphoreType.DMA
    return pl.pallas_call(
        functools.partial(gram_kernel, peers, layers),
        out_shape=(
            jax.ShapeDtypeStruct((mats, share, peers, samples, width), bf16),
            jax.ShapeDtypeStruct((total, total), f32),
            jax.ShapeDtypeStruct((peers, 1, total), f32),
        ),
        in_specs=[pl.BlockSpec(memory_space=pltpu.HBM)] * 4,
        out_specs=(vmem, vmem, vmem),
        scratch_shapes=[
            pltpu.VMEM(spins.shape, jnp.int32),
            pltpu.VMEM((1, samples), f32),
            pltpu.VMEM(activations.shape, bf16),
            pltpu.VMEM(cotangents.shape, bf16),
            pltpu.VMEM((width // 128 * width * samples, 128), f32),
            pltpu.VMEM((mats, peers, share, samples, width), bf16),
            pltpu.VMEM((total, total), f32),
            pltpu.VMEM((peers, samples, total), f32),
            pltpu.VMEM((layers, samples, total), f32),
            pltpu.VMEM((samples, total), f32),
            pltpu.VMEM((1, total), f32),
            dma((2,)),
            dma,
            dma,
            dma((2, samples)),
            dma((mats,)),
            dma((mats,)),
            dma((mats,)),
            dma,
            dma,
            dma((layers,)),
            dma((layers,)),
            dma,
            dma,
        ],
        compiler_params=pltpu.CompilerParams(
            collective_id=0, has_side_effects=True, vmem_limit_bytes=20 << 20
        ),
    )(*(pltpu.with_memory_space_constraint(a, pltpu.HBM) for a in (spins, offdiag[None, :], activations, cotangents)))


def minus_inverse(entry, order):
    at = lambda i, j: entry[min(i, j), max(i, j)]
    for p in range(0, order, 2):
        q = p + 1
        first, cross, second = entry[p, p], entry[p, q], entry[q, q]
        scale = 1.0 / (first * second - cross * cross)
        inv_pp, inv_pq, inv_qq = second * scale, cross * scale, first * scale
        others = [i for i in range(order) if i not in (p, q)]
        gain = {
            i: (
                at(i, p) * inv_pp - at(i, q) * inv_pq,
                at(i, q) * inv_qq - at(i, p) * inv_pq,
            )
            for i in others
        }
        fresh = {}
        for x, i in enumerate(others):
            for j in others[x:]:
                fresh[i, j] = entry[i, j] - (gain[i][0] * at(j, p) + gain[i][1] * at(j, q))
            fresh[min(i, p), max(i, p)] = gain[i][0]
            fresh[min(i, q), max(i, q)] = gain[i][1]
        fresh[p, p], fresh[p, q], fresh[q, q] = -inv_pp, inv_pq, -inv_qq
        entry = fresh
        at = lambda i, j, entry=entry: entry[min(i, j), max(i, j)]
    return entry


def tree_sum(terms):
    while len(terms) > 1:
        terms = [a + b for a, b in zip(terms[::2], terms[1::2], strict=True)]
    return terms[0]


def spread_columns(group, start):
    return [jnp.broadcast_to(group[:, start + j : start + j + 1], group.shape) for j in range(8)]


def sweep(groups, k, own_columns, shelf):
    shape = groups[k].shape
    lane, sub = iota(shape, 1), iota(shape, 0)
    start, slot = 8 * k, k % 2

    def put(place, tiles):
        for j, tile in enumerate(tiles):
            shelf[slot, place + 8 * j : place + 8 * j + 8, :] = tile

    def spread_row(place, j, i):
        return shelf[slot, pl.ds(place + 8 * j + i, 8, stride=0), :]

    put(0, own_columns)
    entry = {(i, j): spread_row(0, j, i) for i in range(8) for j in range(i, 8)}
    entry = minus_inverse(entry, 8)
    at = lambda i, j: entry[min(i, j), max(i, j)]
    next_columns, columns = None, {}
    if start + 8 < shape[1]:
        near = columns[k + 1] = spread_columns(groups[k + 1], start)
        put(64, near)
        gains = [tree_sum([at(i, a) * near[a] for a in range(8)]) for i in range(8)]
        old = spread_columns(groups[k + 1], start + 8)
        next_columns = [
            old[j] + tree_sum([gains[i] * spread_row(64, i, j) for i in range(8)]) for j in range(8)
        ]
    put(128, [groups[k]])
    inside = (lane >= start) & (lane < start + 8)
    marked = [
        jnp.where(inside, jnp.where(lane == start + j, -1.0, 0.0), spread_row(128, 0, j)) for j in range(8)
    ]
    scaled = [tree_sum([at(i, j) * marked[j] for j in range(8)]) for i in range(8)]
    swept = [None] * k
    fresh = -scaled[7]
    for i in range(7):
        fresh = jnp.where(sub == i, -scaled[i], fresh)
    swept.append(fresh)
    for v in range(k + 1, len(groups)):
        spread = columns.get(v) or spread_columns(groups[v], start)
        swept.append(
            jnp.where(inside, 0.0, groups[v]) + tree_sum([spread[i] * scaled[i] for i in range(8)])
        )
    return swept, next_columns


def solve(matrix, lower, scaled_lower, shelf, rhs):
    half = matrix.shape[0] // 2
    dot = functools.partial(jnp.dot, precision=highest, preferred_element_type=f32)
    count = half // 8
    lane = iota((8, half), 1)
    groups = [matrix[8 * v : 8 * v + 8, 0:half] for v in range(count)]
    groups.append(jnp.broadcast_to(rhs[:, 0:half], (8, half)))
    columns = spread_columns(groups[0], 0)
    for k in range(count):
        pivots = groups[k]
        groups, columns = sweep(groups, k, columns, shelf)
        done, own = lane < 8 * k + 8, lane >= 8 * k
        unit = jnp.where(lane == 8 * k + iota((8, half), 0), -1.0, 0.0)
        lower[8 * k : 8 * k + 8, :] = jnp.where(done, jnp.where(own, unit, pivots), 0.0)
        scaled_lower[8 * k : 8 * k + 8, :] = jnp.where(done, groups[k], 0.0)
    top = groups[count]
    cross = dot(
        lax.dot_general(
            matrix[half : 2 * half, 0:half], lower[...], (((1,), (1,)), ((), ())),
            precision=highest, preferred_element_type=f32,
        ),
        scaled_lower[...],
    )
    rest = matrix[half : 2 * half, half : 2 * half] - dot(cross, matrix[0:half, half : 2 * half])
    groups = [rest[8 * v : 8 * v + 8, :] for v in range(count)]
    groups.append(rhs[:, half : 2 * half] - dot(top, matrix[0:half, half : 2 * half]))
    columns = spread_columns(groups[0], 0)
    for k in range(count):
        groups, columns = sweep(groups, k, columns, shelf)
    bottom = groups[count]
    top = top - dot(bottom, cross)
    return jnp.concatenate([top[0:1, :], bottom[0:1, :]], axis=1)


def solve_kernel(rows_ref, gram_ref, energy_ref, weights_ref, update_ref, work, lower, scaled_lower, shelf):
    mats, share, peers, samples, width = rows_ref.shape
    total = peers * samples
    me = lax.axis_index("samp")
    raw = gram_ref[...]
    means = jnp.mean(raw, axis=1, keepdims=True)
    diagonal = iota((total, total), 0) == iota((total, total), 1)

    def as_row(col):
        return jnp.sum(jnp.where(diagonal, col, 0.0), axis=0, keepdims=True)

    means_row = as_row(means)
    gram = (raw - means - means_row + jnp.mean(means_row)) / total
    trace = jnp.sum(jnp.where(diagonal, gram, 0.0))
    work[...] = gram + jnp.where(diagonal, SHIFT_RATIO * trace / total, 0.0)
    every = energy_ref[...].reshape(peers, total)
    held = iota((peers, total), 1) // samples == iota((peers, total), 0)
    energy = jnp.sum(jnp.where(held, every, 0.0), axis=0, keepdims=True)
    eps = (energy - jnp.mean(energy)) / jnp.sqrt(f32(total))
    weights = solve(work, lower, scaled_lower, shelf, eps)
    weights_ref[...] = pltpu.roll(weights, total - me * samples, 1)[:, 0:samples]
    coeffs = weights - jnp.mean(weights)
    first = coeffs.astype(jnp.bfloat16)
    rest = coeffs - first.astype(f32)
    second = rest.astype(jnp.bfloat16)
    third = (rest - second.astype(f32)).astype(jnp.bfloat16)
    split = jnp.concatenate(
        [first.astype(f32), second.astype(f32), third.astype(f32), jnp.zeros((5, total), f32)], axis=0
    ).astype(jnp.bfloat16)
    for m in range(mats):
        for r in range(share):
            rows = rows_ref[m, r].reshape(total, width)
            parts = jnp.dot(split, rows, preferred_element_type=f32)
            update_ref[m, r : r + 1, :] = jnp.sum(parts, axis=0, keepdims=True)


def solve_and_update(rows, gram, energy):
    mats, share, peers, samples, width = rows.shape
    total = peers * samples
    vmem = pl.BlockSpec(memory_space=pltpu.VMEM)
    return pl.pallas_call(
        solve_kernel,
        out_shape=(
            jax.ShapeDtypeStruct((1, samples), f32),
            jax.ShapeDtypeStruct((mats, share, width), f32),
        ),
        in_specs=[vmem, vmem, vmem],
        out_specs=(vmem, vmem),
        scratch_shapes=[
            pltpu.VMEM((total, total), f32),
            pltpu.VMEM((total // 2, total // 2), f32),
            pltpu.VMEM((total // 2, total // 2), f32),
            pltpu.VMEM((2, 136, total // 2), f32),
        ],
        compiler_params=pltpu.CompilerParams(vmem_limit_bytes=20 << 20),
    )(rows, gram, energy)


def body(spins, activations, cotangents, offdiag):
    rows, gram, energy = gram_and_rows(spins, activations, cotangents, offdiag)
    weights, update = solve_and_update(rows, gram, energy)
    return weights[0], update


def solution(mesh):
    placed = (
        P("samp", None),
        P("samp", "layer", None, None),
        P("samp", "layer", None, None),
        P("samp"),
    )
    return jax.shard_map(
        body,
        mesh=mesh,
        in_specs=placed,
        out_specs=(P("samp"), P("layer", "samp", None)),
        check_vma=False,
    )
```

```python
import functools

import jax
import jax.numpy as jnp
from jax import lax
from jax.experimental import pallas as pl
from jax.experimental.pallas import tpu as pltpu
from jax.sharding import PartitionSpec as P

SIDE = 16
SHIFT_RATIO = 0.1
highest = lax.Precision.HIGHEST
MESH = pl.DeviceIdType.MESH
f32 = jnp.float32
CHIPS = (2, 2), (2, 1), (1, 2), (2, 3), (3, 2), (1, 1), (3, 3), (1, 3), (3, 1), (2, 0), (0, 2), (1, 0), (3, 0), (0, 1), (0, 3)
FAR_FIRST = [(y, z, c) for c in (0, 1) for y, z in CHIPS] + [(0, 0, 1)]

CHIP_STEPS = sorted(
    [(y, z, x) for y in range(4) for z in range(4) for x in range(4) if y or z or x],
    key=lambda step: -sum(min(hop, 4 - hop) for hop in step),
)


def peer_at(me, step):
    y, z, core = step
    row, col = me // 8, me // 2 % 4
    return (row + y) % 4 * 8 + (col + z) % 4 * 2 + (me + core) % 2


def iota(shape, dim):
    return lax.broadcasted_iota(jnp.int32, shape, dim)


def local_energy(spins, offdiag_row):
    samples, sites = spins.shape
    z = (2 * spins - 1).astype(f32)
    column = iota((samples, sites), 1) % SIDE
    next_column = jnp.where(
        column == SIDE - 1,
        pltpu.roll(z, SIDE - 1, 1),
        pltpu.roll(z, sites - 1, 1),
    )
    next_row = pltpu.roll(z, sites - SIDE, 1)
    bonds = jnp.sum(z * (next_column + next_row), axis=1, keepdims=True)
    square = jnp.broadcast_to(offdiag_row, (samples, samples))
    diagonal = iota((samples, samples), 0) == iota((samples, samples), 1)
    energy = bonds + jnp.sum(jnp.where(diagonal, square, 0.0), axis=1, keepdims=True)
    repeated = iota((samples, sites), 1) % samples == iota((samples, sites), 0)
    return jnp.sum(jnp.where(repeated, energy, 0.0), axis=0, keepdims=True)


def gram_kernel(
    peers, layers,
    spins_hbm, offdiag_hbm, act_hbm, cot_hbm,
    rows_ref, gram_ref, energy_ref,
    spins, offdiag, act, cot, wide, outgoing, own_gram, pieces, sums, spread, energy,
    small_sem, energy_send, energy_recv,
    planes, in_sem, own_sem, row_send, row_recv, piece_send, piece_recv,
    sum_send, sum_recv, spread_send, spread_recv,
):
    samples, mats, sites, width = act.shape
    share = width // peers
    me = lax.axis_index("samp")
    layer = lax.axis_index("layer")

    def loads(m, s):
        return (
            pltpu.make_async_copy(act_hbm.at[s, m], act.at[s, m], in_sem.at[0, m, s]),
            pltpu.make_async_copy(cot_hbm.at[s, m], cot.at[s, m], in_sem.at[1, m, s]),
        )

    small = (
        pltpu.make_async_copy(spins_hbm, spins, small_sem.at[0]),
        pltpu.make_async_copy(offdiag_hbm, offdiag, small_sem.at[1]),
    )
    steps = [peer_at(me, step) for step in FAR_FIRST]
    barrier = pltpu.get_barrier_semaphore()
    for peer in steps:
        pl.semaphore_signal(barrier, inc=1, device_id={"samp": peer}, device_id_type=MESH)
    others = [lax.rem(layer + i, layers) for i in (2, 1, 3)]
    for other in others:
        pl.semaphore_signal(barrier, inc=1, device_id={"layer": other}, device_id_type=MESH)
    for m in range(mats):
        for s in range(samples):
            for load in loads(m, s):
                load.start()
        if m == 0:
            for load in small:
                load.start()
    for load in small:
        load.wait()
    energy[...] = local_energy(spins[...], offdiag[...])

    def energy_copy(peer):
        return pltpu.make_async_remote_copy(
            src_ref=energy,
            dst_ref=energy_ref.at[me],
            send_sem=energy_send,
            recv_sem=energy_recv,
            device_id={"samp": peer},
            device_id_type=MESH,
        )

    def row_copy(m, peer):
        return pltpu.make_async_remote_copy(
            src_ref=outgoing.at[m, peer],
            dst_ref=rows_ref.at[m, :, me],
            send_sem=row_send.at[m],
            recv_sem=row_recv.at[m],
            device_id={"samp": peer},
            device_id_type=MESH,
        )

    for m in range(mats):
        for s in range(samples):
            for load in loads(m, s):
                load.wait()
            jac = lax.dot_general(
                act[s, m], cot[s, m], (((0,), (0,)), ((), ())), preferred_element_type=f32
            )
            for h in range(width // 128):
                wide[pl.ds(h * width * samples + s, width, stride=samples), :] = jac[:, h * 128 : (h + 1) * 128]
        for h in range(width // 128):
            for k in range(peers):
                start = h * width * samples + k * share * samples
                block = wide[start : start + share * samples, :]
                outgoing[m, k, :, :, h * 128 : (h + 1) * 128] = block.reshape(share, samples, 128).astype(jnp.bfloat16)
        if m == 0:
            pl.semaphore_wait(barrier, peers + layers - 2)
            for other in others:
                pl.semaphore_signal(planes, inc=1, device_id={"layer": other}, device_id_type=MESH)
        for peer in steps:
            row_copy(m, peer).start()
        if m == 0:
            for peer in steps:
                energy_copy(peer).start()
            energy_ref[me] = energy[...]
        pltpu.make_async_copy(outgoing.at[m, me], rows_ref.at[m, :, me], own_sem.at[m]).start()

    for m in range(mats):
        pltpu.make_async_copy(outgoing.at[m, me], rows_ref.at[m, :, me], own_sem.at[m]).wait()
        many = rows_ref.at[m, :, 0 : peers - 1]
        pltpu.make_async_copy(many, many, row_recv.at[m]).wait()
        total = None
        for r in range(share):
            rows = rows_ref[m, r].reshape(peers * samples, width)
            term = lax.dot_general(
                rows, rows, (((1,), (1,)), ((), ())), preferred_element_type=f32
            )
            total = term if total is None else total + term
        for h in range(2):
            part = total[:, h * 128 : (h + 1) * 128]
            own_gram[h] = part if m == 0 else own_gram[h] + part
    pl.semaphore_wait(planes, layers - 1)

    core = me % 2
    chip = me // 2 * layers + layer

    def tile_of(q):
        return q % 2, pl.ds(pl.multiple_of(q // 2 * 8, 8), 8)

    def chip_at(step):
        y, z, x = step
        place = (me // 8 + y) % 4 * 4 + (me // 2 % 4 + z) % 4
        return place * 2 + core, (layer + x) % layers, place * layers + (layer + x) % layers

    chips = [chip_at(step) for step in CHIP_STEPS]

    def piece_copy(samp, plane, q):
        return pltpu.make_async_remote_copy(
            src_ref=own_gram.at[tile_of(q)],
            dst_ref=pieces.at[chip],
            send_sem=piece_send,
            recv_sem=piece_recv,
            device_id={"samp": samp, "layer": plane},
            device_id_type=MESH,
        )

    for samp, plane, q in chips:
        piece_copy(samp, plane, q).start()
    pieces[chip] = own_gram[tile_of(chip)]
    many = pieces.at[0 : len(chips)]
    pltpu.make_async_copy(many, many, piece_recv).wait()
    sums[core] = jnp.sum(pieces[...], axis=0)
    sibling = pltpu.make_async_remote_copy(
        src_ref=sums.at[core],
        dst_ref=sums.at[core],
        send_sem=sum_send,
        recv_sem=sum_recv,
        device_id={"samp": me + 1 - 2 * core},
        device_id_type=MESH,
    )
    sibling.start()
    sibling.wait()
    spread[...] = sums[0] + sums[1]

    def spread_copy(samp, plane):
        return pltpu.make_async_remote_copy(
            src_ref=spread,
            dst_ref=gram_ref.at[tile_of(chip)],
            send_sem=spread_send,
            recv_sem=spread_recv,
            device_id={"samp": samp, "layer": plane},
            device_id_type=MESH,
        )

    for samp, plane, q in chips:
        spread_copy(samp, plane).start()
    gram_ref[tile_of(chip)] = spread[...]
    for m in range(mats):
        many = outgoing.at[m, 0 : peers - 1]
        pltpu.make_async_copy(many, many, row_send.at[m]).wait()
    many = energy_ref.at[0 : peers - 1]
    pltpu.make_async_copy(many, many, energy_send).wait()
    pltpu.make_async_copy(many, many, energy_recv).wait()
    many = pieces.at[0 : len(chips)]
    pltpu.make_async_copy(many, many, piece_send).wait()
    pltpu.make_async_copy(many, many, spread_recv).wait()
    pltpu.make_async_copy(many, many, spread_send).wait()


def gram_and_rows(spins, activations, cotangents, offdiag):
    samples, mats, sites, width = activations.shape
    peers, layers = lax.axis_size("samp"), lax.axis_size("layer")
    total, share = peers * samples, width // peers
    bf16 = jnp.bfloat16
    vmem = pl.BlockSpec(memory_space=pltpu.VMEM)
    dma = pltpu.SemaphoreType.DMA
    return pl.pallas_call(
        functools.partial(gram_kernel, peers, layers),
        out_shape=(
            jax.ShapeDtypeStruct((mats, share, peers, samples, width), bf16),
            jax.ShapeDtypeStruct((2, total, 128), f32),
            jax.ShapeDtypeStruct((peers, 1, total), f32),
        ),
        in_specs=[pl.BlockSpec(memory_space=pltpu.HBM)] * 4,
        out_specs=(vmem, vmem, vmem),
        scratch_shapes=[
            pltpu.VMEM(spins.shape, jnp.int32),
            pltpu.VMEM((1, samples), f32),
            pltpu.VMEM(activations.shape, bf16),
            pltpu.VMEM(cotangents.shape, bf16),
            pltpu.VMEM((width // 128 * width * samples, 128), f32),
            pltpu.VMEM((mats, peers, share, samples, width), bf16),
            pltpu.VMEM((2, total, 128), f32),
            pltpu.VMEM((peers // 2 * layers, 8, 128), f32),
            pltpu.VMEM((2, 8, 128), f32),
            pltpu.VMEM((8, 128), f32),
            pltpu.VMEM((1, total), f32),
            dma((2,)),
            dma,
            dma,
            pltpu.SemaphoreType.REGULAR,
            dma((2, mats, samples)),
            dma((mats,)),
            dma((mats,)),
            dma((mats,)),
            dma,
            dma,
            dma,
            dma,
            dma,
            dma,
        ],
        compiler_params=pltpu.CompilerParams(
            collective_id=0, has_side_effects=True, vmem_limit_bytes=20 << 20
        ),
    )(*(pltpu.with_memory_space_constraint(a, pltpu.HBM) for a in (spins, offdiag[None, :], activations, cotangents)))


def minus_inverse(entry, order):
    at = lambda i, j: entry[min(i, j), max(i, j)]
    for p in range(0, order, 2):
        q = p + 1
        first, cross, second = entry[p, p], entry[p, q], entry[q, q]
        scale = 1.0 / (first * second - cross * cross)
        inv_pp, inv_pq, inv_qq = second * scale, cross * scale, first * scale
        others = [i for i in range(order) if i not in (p, q)]
        gain = {
            i: (
                at(i, p) * inv_pp - at(i, q) * inv_pq,
                at(i, q) * inv_qq - at(i, p) * inv_pq,
            )
            for i in others
        }
        fresh = {}
        for x, i in enumerate(others):
            for j in others[x:]:
                fresh[i, j] = entry[i, j] - (gain[i][0] * at(j, p) + gain[i][1] * at(j, q))
            fresh[min(i, p), max(i, p)] = gain[i][0]
            fresh[min(i, q), max(i, q)] = gain[i][1]
        fresh[p, p], fresh[p, q], fresh[q, q] = -inv_pp, inv_pq, -inv_qq
        entry = fresh
        at = lambda i, j, entry=entry: entry[min(i, j), max(i, j)]
    return entry


def tree_sum(terms):
    while len(terms) > 1:
        terms = [a + b for a, b in zip(terms[::2], terms[1::2], strict=True)]
    return terms[0]


def spread_columns(group, start):
    return [jnp.broadcast_to(group[:, start + j : start + j + 1], group.shape) for j in range(8)]


def sweep(groups, k, own_columns, shelf):
    shape = groups[k].shape
    lane, sub = iota(shape, 1), iota(shape, 0)
    start, slot = 8 * k, k % 2

    def put(place, tiles):
        for j, tile in enumerate(tiles):
            shelf[slot, place + 8 * j : place + 8 * j + 8, :] = tile

    def spread_row(place, j, i):
        return shelf[slot, pl.ds(place + 8 * j + i, 8, stride=0), :]

    put(0, own_columns)
    entry = {(i, j): spread_row(0, j, i) for i in range(8) for j in range(i, 8)}
    entry = minus_inverse(entry, 8)
    at = lambda i, j: entry[min(i, j), max(i, j)]
    next_columns, columns = None, {}
    if start + 8 < shape[1]:
        near = columns[k + 1] = spread_columns(groups[k + 1], start)
        put(64, near)
        gains = [tree_sum([at(i, a) * near[a] for a in range(8)]) for i in range(8)]
        old = spread_columns(groups[k + 1], start + 8)
        next_columns = [
            old[j] + tree_sum([gains[i] * spread_row(64, i, j) for i in range(8)]) for j in range(8)
        ]
    put(128, [groups[k]])
    inside = (lane >= start) & (lane < start + 8)
    marked = [
        jnp.where(inside, jnp.where(lane == start + j, -1.0, 0.0), spread_row(128, 0, j)) for j in range(8)
    ]
    scaled = [tree_sum([at(i, j) * marked[j] for j in range(8)]) for i in range(8)]
    swept = [None] * k
    fresh = -scaled[7]
    for i in range(7):
        fresh = jnp.where(sub == i, -scaled[i], fresh)
    swept.append(fresh)
    for v in range(k + 1, len(groups)):
        spread = columns.get(v) or spread_columns(groups[v], start)
        swept.append(
            jnp.where(inside, 0.0, groups[v]) + tree_sum([spread[i] * scaled[i] for i in range(8)])
        )
    return swept, next_columns


def solve(matrix, lower, scaled_lower, shelf, rhs):
    half = matrix.shape[0] // 2
    dot = functools.partial(jnp.dot, precision=highest, preferred_element_type=f32)
    count = half // 8
    lane = iota((8, half), 1)
    groups = [matrix[8 * v : 8 * v + 8, 0:half] for v in range(count)]
    groups.append(jnp.broadcast_to(rhs[:, 0:half], (8, half)))
    columns = spread_columns(groups[0], 0)
    for k in range(count):
        pivots = groups[k]
        groups, columns = sweep(groups, k, columns, shelf)
        done, own = lane < 8 * k + 8, lane >= 8 * k
        unit = jnp.where(lane == 8 * k + iota((8, half), 0), -1.0, 0.0)
        lower[8 * k : 8 * k + 8, :] = jnp.where(done, jnp.where(own, unit, pivots), 0.0)
        scaled_lower[8 * k : 8 * k + 8, :] = jnp.where(done, groups[k], 0.0)
    top = groups[count]
    cross = dot(
        lax.dot_general(
            matrix[half : 2 * half, 0:half], lower[...], (((1,), (1,)), ((), ())),
            precision=highest, preferred_element_type=f32,
        ),
        scaled_lower[...],
    )
    rest = matrix[half : 2 * half, half : 2 * half] - dot(cross, matrix[0:half, half : 2 * half])
    groups = [rest[8 * v : 8 * v + 8, :] for v in range(count)]
    groups.append(rhs[:, half : 2 * half] - dot(top, matrix[0:half, half : 2 * half]))
    columns = spread_columns(groups[0], 0)
    for k in range(count):
        groups, columns = sweep(groups, k, columns, shelf)
    bottom = groups[count]
    top = top - dot(bottom, cross)
    return jnp.concatenate([top[0:1, :], bottom[0:1, :]], axis=1)


def solve_kernel(rows_ref, gram_ref, energy_ref, weights_ref, update_ref, work, lower, scaled_lower, shelf):
    mats, share, peers, samples, width = rows_ref.shape
    total = peers * samples
    me = lax.axis_index("samp")
    raw = jnp.concatenate([gram_ref[0], gram_ref[1]], axis=1)
    means = jnp.mean(raw, axis=1, keepdims=True)
    diagonal = iota((total, total), 0) == iota((total, total), 1)

    def as_row(col):
        return jnp.sum(jnp.where(diagonal, col, 0.0), axis=0, keepdims=True)

    means_row = as_row(means)
    gram = (raw - means - means_row + jnp.mean(means_row)) / total
    trace = jnp.sum(jnp.where(diagonal, gram, 0.0))
    work[...] = gram + jnp.where(diagonal, SHIFT_RATIO * trace / total, 0.0)
    every = energy_ref[...].reshape(peers, total)
    held = iota((peers, total), 1) // samples == iota((peers, total), 0)
    energy = jnp.sum(jnp.where(held, every, 0.0), axis=0, keepdims=True)
    eps = (energy - jnp.mean(energy)) / jnp.sqrt(f32(total))
    weights = solve(work, lower, scaled_lower, shelf, eps)
    weights_ref[...] = pltpu.roll(weights, total - me * samples, 1)[:, 0:samples]
    coeffs = weights - jnp.mean(weights)
    first = coeffs.astype(jnp.bfloat16)
    rest = coeffs - first.astype(f32)
    second = rest.astype(jnp.bfloat16)
    third = (rest - second.astype(f32)).astype(jnp.bfloat16)
    split = jnp.concatenate(
        [first.astype(f32), second.astype(f32), third.astype(f32), jnp.zeros((5, total), f32)], axis=0
    ).astype(jnp.bfloat16)
    for m in range(mats):
        for r in range(share):
            rows = rows_ref[m, r].reshape(total, width)
            parts = jnp.dot(split, rows, preferred_element_type=f32)
            update_ref[m, r : r + 1, :] = jnp.sum(parts, axis=0, keepdims=True)


def solve_and_update(rows, gram, energy):
    mats, share, peers, samples, width = rows.shape
    total = peers * samples
    vmem = pl.BlockSpec(memory_space=pltpu.VMEM)
    return pl.pallas_call(
        solve_kernel,
        out_shape=(
            jax.ShapeDtypeStruct((1, samples), f32),
            jax.ShapeDtypeStruct((mats, share, width), f32),
        ),
        in_specs=[vmem, vmem, vmem],
        out_specs=(vmem, vmem),
        scratch_shapes=[
            pltpu.VMEM((total, total), f32),
            pltpu.VMEM((total // 2, total // 2), f32),
            pltpu.VMEM((total // 2, total // 2), f32),
            pltpu.VMEM((2, 136, total // 2), f32),
        ],
        compiler_params=pltpu.CompilerParams(vmem_limit_bytes=20 << 20),
    )(rows, gram, energy)


def body(spins, activations, cotangents, offdiag):
    rows, gram, energy = gram_and_rows(spins, activations, cotangents, offdiag)
    weights, update = solve_and_update(rows, gram, energy)
    return weights[0], update


def solution(mesh):
    placed = (
        P("samp", None),
        P("samp", "layer", None, None),
        P("samp", "layer", None, None),
        P("samp"),
    )
    return jax.shard_map(
        body,
        mesh=mesh,
        in_specs=placed,
        out_specs=(P("samp"), P("layer", "samp", None)),
        check_vma=False,
    )
```

```python
import functools

import jax
import jax.numpy as jnp
from jax import lax
from jax.experimental import pallas as pl
from jax.experimental.pallas import tpu as pltpu
from jax.sharding import PartitionSpec as P

SIDE = 16
SHIFT_RATIO = 0.1
highest = lax.Precision.HIGHEST
MESH = pl.DeviceIdType.MESH
f32 = jnp.float32
CHIPS = (2, 2), (2, 1), (1, 2), (2, 3), (3, 2), (1, 1), (3, 3), (1, 3), (3, 1), (2, 0), (0, 2), (1, 0), (3, 0), (0, 1), (0, 3)
FAR_FIRST = [(y, z, c) for c in (0, 1) for y, z in CHIPS] + [(0, 0, 1)]

OWNING = 3


def far_first(steps):
    return sorted(steps, key=lambda step: -sum(min(hop, 4 - hop) for hop in step))


PLACE_STEPS = far_first([(y, z) for y in range(4) for z in range(4) if y or z])
CHIP_STEPS = far_first(
    [(y, z, x) for y in range(4) for z in range(4) for x in range(4) if y or z or x]
)


def peer_at(me, step):
    y, z, core = step
    row, col = me // 8, me // 2 % 4
    return (row + y) % 4 * 8 + (col + z) % 4 * 2 + (me + core) % 2


def iota(shape, dim):
    return lax.broadcasted_iota(jnp.int32, shape, dim)


def local_energy(spins, offdiag_row):
    samples, sites = spins.shape
    z = (2 * spins - 1).astype(f32)
    column = iota((samples, sites), 1) % SIDE
    next_column = jnp.where(
        column == SIDE - 1,
        pltpu.roll(z, SIDE - 1, 1),
        pltpu.roll(z, sites - 1, 1),
    )
    next_row = pltpu.roll(z, sites - SIDE, 1)
    bonds = jnp.sum(z * (next_column + next_row), axis=1, keepdims=True)
    square = jnp.broadcast_to(offdiag_row, (samples, samples))
    diagonal = iota((samples, samples), 0) == iota((samples, samples), 1)
    energy = bonds + jnp.sum(jnp.where(diagonal, square, 0.0), axis=1, keepdims=True)
    repeated = iota((samples, sites), 1) % samples == iota((samples, sites), 0)
    return jnp.sum(jnp.where(repeated, energy, 0.0), axis=0, keepdims=True)


def products(a, b):
    return lax.dot_general(a, b, (((1,), (1,)), ((), ())), preferred_element_type=f32)


def gram_kernel(
    peers, layers,
    spins_hbm, offdiag_hbm, act_hbm, cot_hbm,
    rows_ref, gram_ref, energy_ref,
    spins, offdiag, act, cot, wide, outgoing, own_gram, pieces, sums, spread, energy,
    small_sem, energy_send, energy_recv,
    planes, in_sem, own_sem, row_send, row_recv, piece_send, piece_recv,
    sum_send, sum_recv, spread_send, spread_recv,
):
    samples, mats, sites, width = act.shape
    share = width // peers
    me = lax.axis_index("samp")
    layer = lax.axis_index("layer")

    def loads(m, s):
        return (
            pltpu.make_async_copy(act_hbm.at[s, m], act.at[s, m], in_sem.at[0, m, s]),
            pltpu.make_async_copy(cot_hbm.at[s, m], cot.at[s, m], in_sem.at[1, m, s]),
        )

    small = (
        pltpu.make_async_copy(spins_hbm, spins, small_sem.at[0]),
        pltpu.make_async_copy(offdiag_hbm, offdiag, small_sem.at[1]),
    )
    steps = [peer_at(me, step) for step in FAR_FIRST]
    barrier = pltpu.get_barrier_semaphore()
    for peer in steps:
        pl.semaphore_signal(barrier, inc=1, device_id={"samp": peer}, device_id_type=MESH)
    others = [lax.rem(layer + i, layers) for i in (2, 1, 3)]
    for other in others:
        pl.semaphore_signal(barrier, inc=1, device_id={"layer": other}, device_id_type=MESH)
    for m in range(mats):
        for s in range(samples):
            for load in loads(m, s):
                load.start()
        if m == 0:
            for load in small:
                load.start()
    for load in small:
        load.wait()
    energy[...] = local_energy(spins[...], offdiag[...])

    def energy_copy(peer):
        return pltpu.make_async_remote_copy(
            src_ref=energy,
            dst_ref=energy_ref.at[me],
            send_sem=energy_send,
            recv_sem=energy_recv,
            device_id={"samp": peer},
            device_id_type=MESH,
        )

    def row_copy(m, peer):
        return pltpu.make_async_remote_copy(
            src_ref=outgoing.at[m, peer],
            dst_ref=rows_ref.at[m, :, me],
            send_sem=row_send.at[m],
            recv_sem=row_recv.at[m],
            device_id={"samp": peer},
            device_id_type=MESH,
        )

    for m in range(mats):
        for s in range(samples):
            for load in loads(m, s):
                load.wait()
            jac = lax.dot_general(
                act[s, m], cot[s, m], (((0,), (0,)), ((), ())), preferred_element_type=f32
            )
            for h in range(width // 128):
                wide[pl.ds(h * width * samples + s, width, stride=samples), :] = jac[:, h * 128 : (h + 1) * 128]
        for h in range(width // 128):
            for k in range(peers):
                start = h * width * samples + k * share * samples
                block = wide[start : start + share * samples, :]
                outgoing[m, k, :, :, h * 128 : (h + 1) * 128] = block.reshape(share, samples, 128).astype(jnp.bfloat16)
        if m == 0:
            pl.semaphore_wait(barrier, peers + layers - 2)
            for other in others:
                pl.semaphore_signal(planes, inc=1, device_id={"layer": other}, device_id_type=MESH)
        for peer in steps:
            row_copy(m, peer).start()
        if m == 0:
            for peer in steps:
                energy_copy(peer).start()
            energy_ref[me] = energy[...]
        pltpu.make_async_copy(outgoing.at[m, me], rows_ref.at[m, :, me], own_sem.at[m]).start()

    for m in range(mats):
        pltpu.make_async_copy(outgoing.at[m, me], rows_ref.at[m, :, me], own_sem.at[m]).wait()
        many = rows_ref.at[m, :, 0 : peers - 1]
        pltpu.make_async_copy(many, many, row_recv.at[m]).wait()
        left, right = None, None
        for r in range(share):
            rows = rows_ref[m, r].reshape(peers * samples, width)
            halves = rows[: peers * samples // 2], rows[peers * samples // 2 :]
            first = products(rows, halves[0])
            second = products(halves[1], halves[1])
            left, right = (first, second) if r == 0 else (left + first, right + second)
        parts = jnp.concatenate([left, right], axis=0)
        own_gram[...] = parts if m == 0 else own_gram[...] + parts
    pl.semaphore_wait(planes, layers - 1)

    core = me % 2
    chip = me // 2 * layers + layer

    place = me // 2

    def tile_at(owner_place, plane):
        return pl.ds(pl.multiple_of((owner_place * OWNING + plane) * 8, 8), 8)

    def moved(y, z):
        return (place // 4 + y) % 4 * 4 + (place % 4 + z) % 4

    def piece_copy(there, plane):
        return pltpu.make_async_remote_copy(
            src_ref=own_gram.at[tile_at(there, plane)],
            dst_ref=pieces.at[chip],
            send_sem=piece_send,
            recv_sem=piece_recv,
            device_id={"samp": there * 2 + core, "layer": plane},
            device_id_type=MESH,
        )

    for y, z in PLACE_STEPS:
        for plane in range(OWNING):
            piece_copy(moved(y, z), plane).start()
    for other in others:

        @pl.when(other < OWNING)
        def _(other=other):
            piece_copy(place, other).start()

    def await_tiles(sem, ref, count):
        many = ref.at[0 : count * 8]
        pltpu.make_async_copy(many, many, sem).wait()

    owns = layer < OWNING
    tiles = (peers // 2) * OWNING

    @pl.when(owns)
    def _():
        pieces[chip] = own_gram[tile_at(place, layer)]
        many = pieces.at[0 : len(CHIP_STEPS)]
        pltpu.make_async_copy(many, many, piece_recv).wait()
        sums[core] = jnp.sum(pieces[...], axis=0)
        sibling = pltpu.make_async_remote_copy(
            src_ref=sums.at[core],
            dst_ref=sums.at[core],
            send_sem=sum_send,
            recv_sem=sum_recv,
            device_id={"samp": me + 1 - 2 * core},
            device_id_type=MESH,
        )
        sibling.start()
        sibling.wait()
        spread[...] = sums[0] + sums[1]
        for y, z, x in CHIP_STEPS:
            pltpu.make_async_remote_copy(
                src_ref=spread,
                dst_ref=gram_ref.at[tile_at(place, layer)],
                send_sem=spread_send,
                recv_sem=spread_recv,
                device_id={"samp": moved(y, z) * 2 + core, "layer": (layer + x) % layers},
                device_id_type=MESH,
            ).start()
        gram_ref[tile_at(place, layer)] = spread[...]
        await_tiles(piece_send, own_gram, tiles - 1)
        await_tiles(spread_recv, gram_ref, tiles - 1)
        many = pieces.at[0 : len(CHIP_STEPS)]
        pltpu.make_async_copy(many, many, spread_send).wait()

    @pl.when(jnp.logical_not(owns))
    def _():
        await_tiles(piece_send, own_gram, tiles)
        await_tiles(spread_recv, gram_ref, tiles)

    for m in range(mats):
        many = outgoing.at[m, 0 : peers - 1]
        pltpu.make_async_copy(many, many, row_send.at[m]).wait()
    many = energy_ref.at[0 : peers - 1]
    pltpu.make_async_copy(many, many, energy_send).wait()
    pltpu.make_async_copy(many, many, energy_recv).wait()


def gram_and_rows(spins, activations, cotangents, offdiag):
    samples, mats, sites, width = activations.shape
    peers, layers = lax.axis_size("samp"), lax.axis_size("layer")
    total, share = peers * samples, width // peers
    bf16 = jnp.bfloat16
    vmem = pl.BlockSpec(memory_space=pltpu.VMEM)
    dma = pltpu.SemaphoreType.DMA
    return pl.pallas_call(
        functools.partial(gram_kernel, peers, layers),
        out_shape=(
            jax.ShapeDtypeStruct((mats, share, peers, samples, width), bf16),
            jax.ShapeDtypeStruct((total // 2 * 3, 128), f32),
            jax.ShapeDtypeStruct((peers, 1, total), f32),
        ),
        in_specs=[pl.BlockSpec(memory_space=pltpu.HBM)] * 4,
        out_specs=(vmem, vmem, vmem),
        scratch_shapes=[
            pltpu.VMEM(spins.shape, jnp.int32),
            pltpu.VMEM((1, samples), f32),
            pltpu.VMEM(activations.shape, bf16),
            pltpu.VMEM(cotangents.shape, bf16),
            pltpu.VMEM((width // 128 * width * samples, 128), f32),
            pltpu.VMEM((mats, peers, share, samples, width), bf16),
            pltpu.VMEM((total // 2 * 3, 128), f32),
            pltpu.VMEM((peers // 2 * layers, 8, 128), f32),
            pltpu.VMEM((2, 8, 128), f32),
            pltpu.VMEM((8, 128), f32),
            pltpu.VMEM((1, total), f32),
            dma((2,)),
            dma,
            dma,
            pltpu.SemaphoreType.REGULAR,
            dma((2, mats, samples)),
            dma((mats,)),
            dma((mats,)),
            dma((mats,)),
            dma,
            dma,
            dma,
            dma,
            dma,
            dma,
        ],
        compiler_params=pltpu.CompilerParams(
            collective_id=0, has_side_effects=True, vmem_limit_bytes=20 << 20
        ),
    )(*(pltpu.with_memory_space_constraint(a, pltpu.HBM) for a in (spins, offdiag[None, :], activations, cotangents)))


def eliminate(entry):
    entry = dict(entry)
    inverses, gain = [], {}
    for p in range(0, 8, 2):
        q = p + 1
        first, cross, second = entry[p, p], entry[p, q], entry[q, q]
        scale = 1.0 / (first * second - cross * cross)
        inv = second * scale, cross * scale, first * scale
        inverses.append(inv)
        later = range(p + 2, 8)
        for i in later:
            at_p, at_q = entry[p, i], entry[q, i]
            gain[i, p] = at_p * inv[0] - at_q * inv[1], at_q * inv[2] - at_p * inv[1]
        for i in later:
            for j in range(i, 8):
                entry[i, j] = entry[i, j] - (gain[i, p][0] * entry[p, j] + gain[i, p][1] * entry[q, j])
    return inverses, gain


def forward(gain, values):
    values = list(values)
    for p in range(0, 8, 2):
        for i in range(p + 2, 8):
            by_p, by_q = gain[i, p]
            values[i] = values[i] - (by_p * values[p] + by_q * values[p + 1])
    return values


def scale_pairs(inverses, values):
    scaled = []
    for p in range(0, 8, 2):
        pp, pq, qq = inverses[p // 2]
        first, second = values[p], values[p + 1]
        scaled += [first * pp - second * pq, second * qq - first * pq]
    return scaled


def backward(gain, values):
    values = list(values)
    for p in range(6, -1, -2):
        for i in range(7, p + 1, -1):
            values[p] = values[p] - gain[i, p][0] * values[i]
            values[p + 1] = values[p + 1] - gain[i, p][1] * values[i]
    return values


def tree_sum(terms):
    while len(terms) > 1:
        terms = [a + b for a, b in zip(terms[::2], terms[1::2], strict=True)]
    return terms[0]


def spread_columns(group, start):
    return [jnp.broadcast_to(group[:, start + j : start + j + 1], group.shape) for j in range(8)]


def sweep(groups, k, own_columns, shelf):
    shape = groups[k].shape
    lane, sub = iota(shape, 1), iota(shape, 0)
    start, slot = 8 * k, k % 2

    def put(place, tiles):
        for j, tile in enumerate(tiles):
            shelf[slot, place + 8 * j : place + 8 * j + 8, :] = tile

    def spread_row(place, j, i):
        return shelf[slot, pl.ds(place + 8 * j + i, 8, stride=0), :]

    put(0, own_columns)
    entry = {(i, j): spread_row(0, j, i) for i in range(8) for j in range(i, 8)}
    inverses, gain = eliminate(entry)
    next_columns, columns = None, {}
    if start + 8 < shape[1]:
        near = columns[k + 1] = spread_columns(groups[k + 1], start)
        reduced = forward(gain, near)
        put(64, reduced)
        gains = scale_pairs(inverses, reduced)
        old = spread_columns(groups[k + 1], start + 8)
        next_columns = [
            old[j] - tree_sum([gains[i] * spread_row(64, i, j) for i in range(8)]) for j in range(8)
        ]
    put(128, [groups[k]])
    inside = (lane >= start) & (lane < start + 8)
    marked = [
        jnp.where(inside, jnp.where(lane == start + j, -1.0, 0.0), spread_row(128, 0, j)) for j in range(8)
    ]
    scaled = backward(gain, scale_pairs(inverses, forward(gain, marked)))
    swept = [None] * k
    fresh = scaled[7]
    for i in range(7):
        fresh = jnp.where(sub == i, scaled[i], fresh)
    swept.append(fresh)
    for v in range(k + 1, len(groups)):
        spread = columns.get(v) or spread_columns(groups[v], start)
        swept.append(
            jnp.where(inside, 0.0, groups[v]) - tree_sum([spread[i] * scaled[i] for i in range(8)])
        )
    return swept, next_columns


def solve(matrix, lower, scaled_lower, shelf, rhs):
    half = matrix.shape[0] // 2
    dot = functools.partial(jnp.dot, precision=highest, preferred_element_type=f32)
    count = half // 8
    lane = iota((8, half), 1)
    groups = [matrix[8 * v : 8 * v + 8, 0:half] for v in range(count)]
    groups.append(jnp.broadcast_to(rhs[:, 0:half], (8, half)))
    columns = spread_columns(groups[0], 0)
    for k in range(count):
        pivots = groups[k]
        groups, columns = sweep(groups, k, columns, shelf)
        done, own = lane < 8 * k + 8, lane >= 8 * k
        unit = jnp.where(lane == 8 * k + iota((8, half), 0), -1.0, 0.0)
        lower[8 * k : 8 * k + 8, :] = jnp.where(done, jnp.where(own, unit, pivots), 0.0)
        scaled_lower[8 * k : 8 * k + 8, :] = jnp.where(done, groups[k], 0.0)
    top = groups[count]
    cross = dot(
        lax.dot_general(
            matrix[half : 2 * half, 0:half], lower[...], (((1,), (1,)), ((), ())),
            precision=highest, preferred_element_type=f32,
        ),
        scaled_lower[...],
    )
    rest = matrix[half : 2 * half, half : 2 * half] - dot(cross, matrix[0:half, half : 2 * half])
    groups = [rest[8 * v : 8 * v + 8, :] for v in range(count)]
    groups.append(rhs[:, half : 2 * half] - dot(top, matrix[0:half, half : 2 * half]))
    columns = spread_columns(groups[0], 0)
    for k in range(count):
        groups, columns = sweep(groups, k, columns, shelf)
    bottom = groups[count]
    top = top - dot(bottom, cross)
    return jnp.concatenate([top[0:1, :], bottom[0:1, :]], axis=1)


def solve_kernel(rows_ref, gram_ref, energy_ref, weights_ref, update_ref, work, lower, scaled_lower, shelf):
    mats, share, peers, samples, width = rows_ref.shape
    total = peers * samples
    me = lax.axis_index("samp")
    half = total // 2
    corner = gram_ref[half:total, :]
    raw = jnp.concatenate(
        [
            jnp.concatenate([gram_ref[0:half, :], corner.T], axis=1),
            jnp.concatenate([corner, gram_ref[total:, :]], axis=1),
        ],
        axis=0,
    )
    means = jnp.mean(raw, axis=1, keepdims=True)
    diagonal = iota((total, total), 0) == iota((total, total), 1)

    def as_row(col):
        return jnp.sum(jnp.where(diagonal, col, 0.0), axis=0, keepdims=True)

    means_row = as_row(means)
    gram = (raw - means - means_row + jnp.mean(means_row)) / total
    trace = jnp.sum(jnp.where(diagonal, gram, 0.0))
    work[...] = gram + jnp.where(diagonal, SHIFT_RATIO * trace / total, 0.0)
    every = energy_ref[...].reshape(peers, total)
    held = iota((peers, total), 1) // samples == iota((peers, total), 0)
    energy = jnp.sum(jnp.where(held, every, 0.0), axis=0, keepdims=True)
    eps = (energy - jnp.mean(energy)) / jnp.sqrt(f32(total))
    weights = solve(work, lower, scaled_lower, shelf, eps)
    weights_ref[...] = pltpu.roll(weights, total - me * samples, 1)[:, 0:samples]
    coeffs = weights - jnp.mean(weights)
    first = coeffs.astype(jnp.bfloat16)
    rest = coeffs - first.astype(f32)
    second = rest.astype(jnp.bfloat16)
    third = (rest - second.astype(f32)).astype(jnp.bfloat16)
    split = jnp.concatenate(
        [first.astype(f32), second.astype(f32), third.astype(f32), jnp.zeros((5, total), f32)], axis=0
    ).astype(jnp.bfloat16)
    for m in range(mats):
        for r in range(share):
            rows = rows_ref[m, r].reshape(total, width)
            parts = jnp.dot(split, rows, preferred_element_type=f32)
            update_ref[m, r : r + 1, :] = jnp.sum(parts, axis=0, keepdims=True)


def solve_and_update(rows, gram, energy):
    mats, share, peers, samples, width = rows.shape
    total = peers * samples
    vmem = pl.BlockSpec(memory_space=pltpu.VMEM)
    return pl.pallas_call(
        solve_kernel,
        out_shape=(
            jax.ShapeDtypeStruct((1, samples), f32),
            jax.ShapeDtypeStruct((mats, share, width), f32),
        ),
        in_specs=[vmem, vmem, vmem],
        out_specs=(vmem, vmem),
        scratch_shapes=[
            pltpu.VMEM((total, total), f32),
            pltpu.VMEM((total // 2, total // 2), f32),
            pltpu.VMEM((total // 2, total // 2), f32),
            pltpu.VMEM((2, 136, total // 2), f32),
        ],
        compiler_params=pltpu.CompilerParams(vmem_limit_bytes=20 << 20),
    )(rows, gram, energy)


def body(spins, activations, cotangents, offdiag):
    rows, gram, energy = gram_and_rows(spins, activations, cotangents, offdiag)
    weights, update = solve_and_update(rows, gram, energy)
    return weights[0], update


def solution(mesh):
    placed = (
        P("samp", None),
        P("samp", "layer", None, None),
        P("samp", "layer", None, None),
        P("samp"),
    )
    return jax.shard_map(
        body,
        mesh=mesh,
        in_specs=placed,
        out_specs=(P("samp"), P("layer", "samp", None)),
        check_vma=False,
    )
```

```python
import functools

import jax
import jax.numpy as jnp
from jax import lax
from jax.experimental import pallas as pl
from jax.experimental.pallas import tpu as pltpu
from jax.sharding import PartitionSpec as P

SIDE = 16
SHIFT_RATIO = 0.1
highest = lax.Precision.HIGHEST
MESH = pl.DeviceIdType.MESH
f32 = jnp.float32
CHIPS = (2, 2), (2, 1), (1, 2), (2, 3), (3, 2), (1, 1), (3, 3), (1, 3), (3, 1), (2, 0), (0, 2), (1, 0), (3, 0), (0, 1), (0, 3)
FAR_FIRST = [(y, z, c) for c in (0, 1) for y, z in CHIPS] + [(0, 0, 1)]

OWNING = 3


def far_first(steps):
    return sorted(steps, key=lambda step: -sum(min(hop, 4 - hop) for hop in step))


PLACE_STEPS = far_first([(y, z) for y in range(4) for z in range(4) if y or z])
CHIP_STEPS = far_first(
    [(y, z, x) for y in range(4) for z in range(4) for x in range(4) if y or z or x]
)


def peer_at(me, step):
    y, z, core = step
    row, col = me // 8, me // 2 % 4
    return (row + y) % 4 * 8 + (col + z) % 4 * 2 + (me + core) % 2


def iota(shape, dim):
    return lax.broadcasted_iota(jnp.int32, shape, dim)


def local_energy(spins, offdiag_row):
    samples, sites = spins.shape
    z = (2 * spins - 1).astype(f32)
    column = iota((samples, sites), 1) % SIDE
    next_column = jnp.where(
        column == SIDE - 1,
        pltpu.roll(z, SIDE - 1, 1),
        pltpu.roll(z, sites - 1, 1),
    )
    next_row = pltpu.roll(z, sites - SIDE, 1)
    bonds = jnp.sum(z * (next_column + next_row), axis=1, keepdims=True)
    square = jnp.broadcast_to(offdiag_row, (samples, samples))
    diagonal = iota((samples, samples), 0) == iota((samples, samples), 1)
    energy = bonds + jnp.sum(jnp.where(diagonal, square, 0.0), axis=1, keepdims=True)
    repeated = iota((samples, sites), 1) % samples == iota((samples, sites), 0)
    return jnp.sum(jnp.where(repeated, energy, 0.0), axis=0, keepdims=True)


def whole_rows(rows_ref, m, r):
    _, halves, peers, _, samples, lanes = rows_ref.shape
    return jnp.concatenate(
        [rows_ref[m, h, :, r].reshape(peers * samples, lanes) for h in range(halves)], axis=1
    )


def products(a, b):
    return lax.dot_general(a, b, (((1,), (1,)), ((), ())), preferred_element_type=f32)


def gram_kernel(
    peers, layers,
    spins_hbm, offdiag_hbm, act_hbm, cot_hbm,
    rows_ref, gram_ref, energy_ref,
    spins, offdiag, act, cot, wide, outgoing, own_gram, pieces, spread, energy,
    small_sem, energy_send, energy_recv,
    planes, in_sem, own_sem, row_send, row_recv, piece_send, piece_recv,
    spread_send, spread_recv,
):
    samples, mats, sites, width = act.shape
    share = width // peers
    halves_of_rows = width // 128
    parts_of_rows = [(m, h) for m in range(mats) for h in range(halves_of_rows)]
    me = lax.axis_index("samp")
    layer = lax.axis_index("layer")

    def loads(m, s):
        return (
            pltpu.make_async_copy(act_hbm.at[s, m], act.at[s, m], in_sem.at[0, m, s]),
            pltpu.make_async_copy(cot_hbm.at[s, m], cot.at[s, m], in_sem.at[1, m, s]),
        )

    small = (
        pltpu.make_async_copy(spins_hbm, spins, small_sem.at[0]),
        pltpu.make_async_copy(offdiag_hbm, offdiag, small_sem.at[1]),
    )
    steps = [peer_at(me, step) for step in FAR_FIRST]
    for m in range(mats):
        for s in range(samples):
            for load in loads(m, s):
                load.start()
        if m == 0:
            for load in small:
                load.start()
    barrier = pltpu.get_barrier_semaphore()
    for peer in steps:
        pl.semaphore_signal(barrier, inc=1, device_id={"samp": peer}, device_id_type=MESH)
    others = [lax.rem(layer + i, layers) for i in (2, 1, 3)]
    for other in others:
        pl.semaphore_signal(barrier, inc=1, device_id={"layer": other}, device_id_type=MESH)
    for load in small:
        load.wait()
    energy[...] = local_energy(spins[...], offdiag[...])

    def energy_copy(peer):
        return pltpu.make_async_remote_copy(
            src_ref=energy,
            dst_ref=energy_ref.at[me],
            send_sem=energy_send,
            recv_sem=energy_recv,
            device_id={"samp": peer},
            device_id_type=MESH,
        )

    def row_copy(m, h, peer):
        return pltpu.make_async_remote_copy(
            src_ref=outgoing.at[m, h, peer],
            dst_ref=rows_ref.at[m, h, me],
            send_sem=row_send.at[m, h],
            recv_sem=row_recv.at[m, h],
            device_id={"samp": peer},
            device_id_type=MESH,
        )

    def keep(m, h):
        return pltpu.make_async_copy(outgoing.at[m, h, me], rows_ref.at[m, h, me], own_sem.at[m, h])

    for m, h in parts_of_rows:
        for s in range(samples):
            if h == 0:
                for load in loads(m, s):
                    load.wait()
            jac = lax.dot_general(
                act[s, m], cot[s, m, :, h * 128 : (h + 1) * 128], (((0,), (0,)), ((), ())),
                preferred_element_type=f32,
            )
            wide[pl.ds(h * width * samples + s, width, stride=samples), :] = jac
        for k in range(peers):
            start = h * width * samples + k * share * samples
            block = wide[start : start + share * samples, :]
            outgoing[m, h, k] = block.reshape(share, samples, 128).astype(jnp.bfloat16)
        if (m, h) == (0, 0):
            pl.semaphore_wait(barrier, peers + layers - 2)
            for other in others:
                pl.semaphore_signal(planes, inc=1, device_id={"layer": other}, device_id_type=MESH)
        for peer in steps[::-1] if m == 0 else steps:
            row_copy(m, h, peer).start()
        keep(m, h).start()
    for peer in steps:
        energy_copy(peer).start()
    energy_ref[me] = energy[...]

    for m in range(mats):
        for h in range(halves_of_rows):
            keep(m, h).wait()
            many = rows_ref.at[m, h, 0 : peers - 1]
            pltpu.make_async_copy(many, many, row_recv.at[m, h]).wait()
        left, right = None, None
        for r in range(share):
            rows = whole_rows(rows_ref, m, r)
            halves = rows[: peers * samples // 2], rows[peers * samples // 2 :]
            first = products(rows, halves[0])
            second = products(halves[1], halves[1])
            left, right = (first, second) if r == 0 else (left + first, right + second)
        parts = jnp.concatenate([left, right], axis=0)
        own_gram[...] = parts if m == 0 else own_gram[...] + parts
    pl.semaphore_wait(planes, layers - 1)

    core = me % 2
    device = me * layers + layer

    place = me // 2

    def tile_at(owner_place, plane):
        return pl.ds(pl.multiple_of((owner_place * OWNING + plane) * 8, 8), 8)

    def moved(y, z):
        return (place // 4 + y) % 4 * 4 + (place % 4 + z) % 4

    def owning_core(there, plane):
        return (there * OWNING + plane) % 2

    def piece_copy(there, plane):
        return pltpu.make_async_remote_copy(
            src_ref=own_gram.at[tile_at(there, plane)],
            dst_ref=pieces.at[device],
            send_sem=piece_send,
            recv_sem=piece_recv,
            device_id={"samp": there * 2 + owning_core(there, plane), "layer": plane},
            device_id_type=MESH,
        )

    for y, z in PLACE_STEPS:
        for plane in range(OWNING):
            piece_copy(moved(y, z), plane).start()
    for other in others:

        @pl.when(other < OWNING)
        def _(other=other):
            piece_copy(place, other).start()

    mine = core == owning_core(place, layer)

    @pl.when((layer < OWNING) & jnp.logical_not(mine))
    def _():
        piece_copy(place, layer).start()

    def await_tiles(sem, ref, count):
        many = ref.at[0 : count * 8]
        pltpu.make_async_copy(many, many, sem).wait()

    owns = (layer < OWNING) & mine
    tiles = (peers // 2) * OWNING
    rest = peers * layers - 1

    @pl.when(owns)
    def _():
        pieces[device] = own_gram[tile_at(place, layer)]
        many = pieces.at[0:rest]
        pltpu.make_async_copy(many, many, piece_recv).wait()
        spread[...] = jnp.sum(pieces[...], axis=0)
        targets = [
            (moved(y, z) * 2 + c, (layer + x) % layers) for y, z, x in CHIP_STEPS for c in range(2)
        ]
        for samp, plane in targets + [(me + 1 - 2 * core, layer)]:
            pltpu.make_async_remote_copy(
                src_ref=spread,
                dst_ref=gram_ref.at[tile_at(place, layer)],
                send_sem=spread_send,
                recv_sem=spread_recv,
                device_id={"samp": samp, "layer": plane},
                device_id_type=MESH,
            ).start()
        gram_ref[tile_at(place, layer)] = spread[...]
        await_tiles(piece_send, own_gram, tiles - 1)
        await_tiles(spread_recv, gram_ref, tiles - 1)
        pltpu.make_async_copy(many, many, spread_send).wait()

    @pl.when(jnp.logical_not(owns))
    def _():
        await_tiles(piece_send, own_gram, tiles)
        await_tiles(spread_recv, gram_ref, tiles)

    for m, h in parts_of_rows:
        many = outgoing.at[m, h, 0 : peers - 1]
        pltpu.make_async_copy(many, many, row_send.at[m, h]).wait()
    many = energy_ref.at[0 : peers - 1]
    pltpu.make_async_copy(many, many, energy_send).wait()
    pltpu.make_async_copy(many, many, energy_recv).wait()


def gram_and_rows(spins, activations, cotangents, offdiag):
    samples, mats, sites, width = activations.shape
    peers, layers = lax.axis_size("samp"), lax.axis_size("layer")
    total, share = peers * samples, width // peers
    bf16 = jnp.bfloat16
    vmem = pl.BlockSpec(memory_space=pltpu.VMEM)
    dma = pltpu.SemaphoreType.DMA
    return pl.pallas_call(
        functools.partial(gram_kernel, peers, layers),
        out_shape=(
            jax.ShapeDtypeStruct((mats, width // 128, peers, share, samples, 128), bf16),
            jax.ShapeDtypeStruct((total // 2 * 3, 128), f32),
            jax.ShapeDtypeStruct((peers, 1, total), f32),
        ),
        in_specs=[pl.BlockSpec(memory_space=pltpu.HBM)] * 4,
        out_specs=(vmem, vmem, vmem),
        scratch_shapes=[
            pltpu.VMEM(spins.shape, jnp.int32),
            pltpu.VMEM((1, samples), f32),
            pltpu.VMEM(activations.shape, bf16),
            pltpu.VMEM(cotangents.shape, bf16),
            pltpu.VMEM((width // 128 * width * samples, 128), f32),
            pltpu.VMEM((mats, width // 128, peers, share, samples, 128), bf16),
            pltpu.VMEM((total // 2 * 3, 128), f32),
            pltpu.VMEM((peers * layers, 8, 128), f32),
            pltpu.VMEM((8, 128), f32),
            pltpu.VMEM((1, total), f32),
            dma((2,)),
            dma,
            dma,
            pltpu.SemaphoreType.REGULAR,
            dma((2, mats, samples)),
            dma((mats, width // 128)),
            dma((mats, width // 128)),
            dma((mats, width // 128)),
            dma,
            dma,
            dma,
            dma,
        ],
        compiler_params=pltpu.CompilerParams(
            collective_id=0, has_side_effects=True, vmem_limit_bytes=20 << 20
        ),
    )(*(pltpu.with_memory_space_constraint(a, pltpu.HBM) for a in (spins, offdiag[None, :], activations, cotangents)))


def eliminate(entry):
    entry = dict(entry)
    inverses, gain = [], {}
    for p in range(0, 8, 2):
        q = p + 1
        first, cross, second = entry[p, p], entry[p, q], entry[q, q]
        scale = 1.0 / (first * second - cross * cross)
        inv = second * scale, cross * scale, first * scale
        inverses.append(inv)
        later = range(p + 2, 8)
        for i in later:
            at_p, at_q = entry[p, i], entry[q, i]
            gain[i, p] = at_p * inv[0] - at_q * inv[1], at_q * inv[2] - at_p * inv[1]
        for i in later:
            for j in range(i, 8):
                entry[i, j] = entry[i, j] - (gain[i, p][0] * entry[p, j] + gain[i, p][1] * entry[q, j])
    return inverses, gain


def forward(gain, values):
    values = list(values)
    for p in range(0, 8, 2):
        for i in range(p + 2, 8):
            by_p, by_q = gain[i, p]
            values[i] = values[i] - (by_p * values[p] + by_q * values[p + 1])
    return values


def scale_pairs(inverses, values):
    scaled = []
    for p in range(0, 8, 2):
        pp, pq, qq = inverses[p // 2]
        first, second = values[p], values[p + 1]
        scaled += [first * pp - second * pq, second * qq - first * pq]
    return scaled


def backward(gain, values):
    values = list(values)
    for p in range(6, -1, -2):
        for i in range(7, p + 1, -1):
            values[p] = values[p] - gain[i, p][0] * values[i]
            values[p + 1] = values[p + 1] - gain[i, p][1] * values[i]
    return values


def tree_sum(terms):
    while len(terms) > 1:
        terms = [a + b for a, b in zip(terms[::2], terms[1::2], strict=True)]
    return terms[0]


def spread_columns(group, start):
    return [jnp.broadcast_to(group[:, start + j : start + j + 1], group.shape) for j in range(8)]


def sweep(groups, k, own_columns, shelf):
    shape = groups[k].shape
    lane, sub = iota(shape, 1), iota(shape, 0)
    start, slot = 8 * k, k % 2

    def put(place, tiles):
        for j, tile in enumerate(tiles):
            shelf[slot, place + 8 * j : place + 8 * j + 8, :] = tile

    def spread_row(place, j, i):
        return shelf[slot, pl.ds(place + 8 * j + i, 8, stride=0), :]

    put(0, own_columns)
    entry = {(i, j): spread_row(0, j, i) for i in range(8) for j in range(i, 8)}
    inverses, gain = eliminate(entry)
    next_columns, columns = None, {}
    if start + 8 < shape[1]:
        near = columns[k + 1] = spread_columns(groups[k + 1], start)
        reduced = forward(gain, near)
        put(64, reduced)
        gains = scale_pairs(inverses, reduced)
        old = spread_columns(groups[k + 1], start + 8)
        next_columns = [
            old[j] - tree_sum([gains[i] * spread_row(64, i, j) for i in range(8)]) for j in range(8)
        ]
    put(128, [groups[k]])
    inside = (lane >= start) & (lane < start + 8)
    marked = [
        jnp.where(inside, jnp.where(lane == start + j, -1.0, 0.0), spread_row(128, 0, j)) for j in range(8)
    ]
    scaled = backward(gain, scale_pairs(inverses, forward(gain, marked)))
    swept = [None] * k
    fresh = scaled[7]
    for i in range(7):
        fresh = jnp.where(sub == i, scaled[i], fresh)
    swept.append(fresh)
    for v in range(k + 1, len(groups)):
        spread = columns.get(v) or spread_columns(groups[v], start)
        swept.append(
            jnp.where(inside, 0.0, groups[v]) - tree_sum([spread[i] * scaled[i] for i in range(8)])
        )
    return swept, next_columns


def solve(matrix, lower, scaled_lower, shelf, rhs):
    half = matrix.shape[0] // 2
    dot = functools.partial(jnp.dot, precision=highest, preferred_element_type=f32)
    count = half // 8
    lane = iota((8, half), 1)
    groups = [matrix[8 * v : 8 * v + 8, 0:half] for v in range(count)]
    groups.append(jnp.broadcast_to(rhs[:, 0:half], (8, half)))
    columns = spread_columns(groups[0], 0)
    for k in range(count):
        pivots = groups[k]
        groups, columns = sweep(groups, k, columns, shelf)
        done, own = lane < 8 * k + 8, lane >= 8 * k
        unit = jnp.where(lane == 8 * k + iota((8, half), 0), -1.0, 0.0)
        lower[8 * k : 8 * k + 8, :] = jnp.where(done, jnp.where(own, unit, pivots), 0.0)
        scaled_lower[8 * k : 8 * k + 8, :] = jnp.where(done, groups[k], 0.0)
    top = groups[count]
    cross = dot(
        lax.dot_general(
            matrix[half : 2 * half, 0:half], lower[...], (((1,), (1,)), ((), ())),
            precision=highest, preferred_element_type=f32,
        ),
        scaled_lower[...],
    )
    rest = matrix[half : 2 * half, half : 2 * half] - dot(cross, matrix[0:half, half : 2 * half])
    groups = [rest[8 * v : 8 * v + 8, :] for v in range(count)]
    groups.append(rhs[:, half : 2 * half] - dot(top, matrix[0:half, half : 2 * half]))
    columns = spread_columns(groups[0], 0)
    for k in range(count):
        groups, columns = sweep(groups, k, columns, shelf)
    bottom = groups[count]
    top = top - dot(bottom, cross)
    return jnp.concatenate([top[0:1, :], bottom[0:1, :]], axis=1)


def solve_kernel(rows_ref, gram_ref, energy_ref, weights_ref, update_ref, work, lower, scaled_lower, shelf):
    mats, halves, peers, share, samples, lanes = rows_ref.shape
    total = peers * samples
    me = lax.axis_index("samp")
    half = total // 2
    corner = gram_ref[half:total, :]
    raw = jnp.concatenate(
        [
            jnp.concatenate([gram_ref[0:half, :], corner.T], axis=1),
            jnp.concatenate([corner, gram_ref[total:, :]], axis=1),
        ],
        axis=0,
    )
    means = jnp.mean(raw, axis=1, keepdims=True)
    diagonal = iota((total, total), 0) == iota((total, total), 1)

    def as_row(col):
        return jnp.sum(jnp.where(diagonal, col, 0.0), axis=0, keepdims=True)

    means_row = as_row(means)
    gram = (raw - means - means_row + jnp.mean(means_row)) / total
    trace = jnp.sum(jnp.where(diagonal, gram, 0.0))
    work[...] = gram + jnp.where(diagonal, SHIFT_RATIO * trace / total, 0.0)
    every = energy_ref[...].reshape(peers, total)
    held = iota((peers, total), 1) // samples == iota((peers, total), 0)
    energy = jnp.sum(jnp.where(held, every, 0.0), axis=0, keepdims=True)
    eps = (energy - jnp.mean(energy)) / jnp.sqrt(f32(total))
    weights = solve(work, lower, scaled_lower, shelf, eps)
    weights_ref[...] = pltpu.roll(weights, total - me * samples, 1)[:, 0:samples]
    coeffs = weights - jnp.mean(weights)
    first = coeffs.astype(jnp.bfloat16)
    rest = coeffs - first.astype(f32)
    second = rest.astype(jnp.bfloat16)
    third = (rest - second.astype(f32)).astype(jnp.bfloat16)
    split = jnp.concatenate(
        [first.astype(f32), second.astype(f32), third.astype(f32), jnp.zeros((5, total), f32)], axis=0
    ).astype(jnp.bfloat16)
    for m in range(mats):
        for r in range(share):
            rows = whole_rows(rows_ref, m, r)
            parts = jnp.dot(split, rows, preferred_element_type=f32)
            update_ref[m, r : r + 1, :] = jnp.sum(parts, axis=0, keepdims=True)


def solve_and_update(rows, gram, energy):
    mats, halves, peers, share, samples, lanes = rows.shape
    width = halves * lanes
    total = peers * samples
    vmem = pl.BlockSpec(memory_space=pltpu.VMEM)
    return pl.pallas_call(
        solve_kernel,
        out_shape=(
            jax.ShapeDtypeStruct((1, samples), f32),
            jax.ShapeDtypeStruct((mats, share, width), f32),
        ),
        in_specs=[vmem, vmem, vmem],
        out_specs=(vmem, vmem),
        scratch_shapes=[
            pltpu.VMEM((total, total), f32),
            pltpu.VMEM((total // 2, total // 2), f32),
            pltpu.VMEM((total // 2, total // 2), f32),
            pltpu.VMEM((2, 136, total // 2), f32),
        ],
        compiler_params=pltpu.CompilerParams(vmem_limit_bytes=20 << 20),
    )(rows, gram, energy)


def body(spins, activations, cotangents, offdiag):
    rows, gram, energy = gram_and_rows(spins, activations, cotangents, offdiag)
    weights, update = solve_and_update(rows, gram, energy)
    return weights[0], update


def solution(mesh):
    placed = (
        P("samp", None),
        P("samp", "layer", None, None),
        P("samp", "layer", None, None),
        P("samp"),
    )
    return jax.shard_map(
        body,
        mesh=mesh,
        in_specs=placed,
        out_specs=(P("samp"), P("layer", "samp", None)),
        check_vma=False,
    )
```

```python
import functools

import jax
import jax.numpy as jnp
from jax import lax
from jax.experimental import pallas as pl
from jax.experimental.pallas import tpu as pltpu
from jax.sharding import PartitionSpec as P

SIDE = 16
SHIFT_RATIO = 0.1
highest = lax.Precision.HIGHEST
MESH = pl.DeviceIdType.MESH
f32 = jnp.float32
CHIPS = (2, 2), (2, 1), (1, 2), (2, 3), (3, 2), (1, 1), (3, 3), (1, 3), (3, 1), (2, 0), (0, 2), (1, 0), (3, 0), (0, 1), (0, 3)
FAR_FIRST = [(y, z, c) for c in (0, 1) for y, z in CHIPS] + [(0, 0, 1)]

OWNING = 3


def far_first(steps):
    return sorted(steps, key=lambda step: -sum(min(hop, 4 - hop) for hop in step))


PLACE_STEPS = far_first([(y, z) for y in range(4) for z in range(4) if y or z])
CHIP_STEPS = far_first(
    [(y, z, x) for y in range(4) for z in range(4) for x in range(4) if y or z or x]
)


def peer_at(me, step):
    y, z, core = step
    row, col = me // 8, me // 2 % 4
    return (row + y) % 4 * 8 + (col + z) % 4 * 2 + (me + core) % 2


def iota(shape, dim):
    return lax.broadcasted_iota(jnp.int32, shape, dim)


def local_energy(spins, offdiag_row):
    samples, sites = spins.shape
    z = (2 * spins - 1).astype(f32)
    column = iota((samples, sites), 1) % SIDE
    next_column = jnp.where(
        column == SIDE - 1,
        pltpu.roll(z, SIDE - 1, 1),
        pltpu.roll(z, sites - 1, 1),
    )
    next_row = pltpu.roll(z, sites - SIDE, 1)
    bonds = jnp.sum(z * (next_column + next_row), axis=1, keepdims=True)
    square = jnp.broadcast_to(offdiag_row, (samples, samples))
    diagonal = iota((samples, samples), 0) == iota((samples, samples), 1)
    energy = bonds + jnp.sum(jnp.where(diagonal, square, 0.0), axis=1, keepdims=True)
    repeated = iota((samples, sites), 1) % samples == iota((samples, sites), 0)
    return jnp.sum(jnp.where(repeated, energy, 0.0), axis=0, keepdims=True)


def whole_rows(rows_ref, m, r):
    _, halves, peers, _, samples, lanes = rows_ref.shape
    return jnp.concatenate(
        [rows_ref[m, h, :, r].reshape(peers * samples, lanes) for h in range(halves)], axis=1
    )


def products(a, b):
    return lax.dot_general(a, b, (((1,), (1,)), ((), ())), preferred_element_type=f32)


def gram_kernel(
    peers, layers,
    spins_hbm, offdiag_hbm, act_hbm, cot_hbm,
    rows_ref, gram_ref, energy_ref,
    spins, offdiag, act, cot, wide, outgoing, own_gram, pieces, spread, energy,
    small_sem, energy_send, energy_recv,
    planes, in_sem, own_sem, row_send, row_recv, piece_send, piece_recv,
    spread_send, spread_recv,
):
    samples, mats, sites, width = act.shape
    share = width // peers
    halves_of_rows = width // 128
    parts_of_rows = [(m, h) for m in range(mats) for h in range(halves_of_rows)]
    me = lax.axis_index("samp")
    layer = lax.axis_index("layer")

    def loads(m, s):
        return (
            pltpu.make_async_copy(act_hbm.at[s, m], act.at[s, m], in_sem.at[0, m, s]),
            pltpu.make_async_copy(cot_hbm.at[s, m], cot.at[s, m], in_sem.at[1, m, s]),
        )

    small = (
        pltpu.make_async_copy(spins_hbm, spins, small_sem.at[0]),
        pltpu.make_async_copy(offdiag_hbm, offdiag, small_sem.at[1]),
    )
    steps = [peer_at(me, step) for step in FAR_FIRST]
    for m in range(mats):
        for s in range(samples):
            for load in loads(m, s):
                load.start()
        if m == 0:
            for load in small:
                load.start()
    barrier = pltpu.get_barrier_semaphore()
    for peer in steps:
        pl.semaphore_signal(barrier, inc=1, device_id={"samp": peer}, device_id_type=MESH)
    others = [lax.rem(layer + i, layers) for i in (2, 1, 3)]
    for other in others:
        pl.semaphore_signal(barrier, inc=1, device_id={"layer": other}, device_id_type=MESH)
    for load in small:
        load.wait()
    energy[...] = local_energy(spins[...], offdiag[...])

    def energy_copy(peer):
        return pltpu.make_async_remote_copy(
            src_ref=energy,
            dst_ref=energy_ref.at[me],
            send_sem=energy_send,
            recv_sem=energy_recv,
            device_id={"samp": peer},
            device_id_type=MESH,
        )

    def row_copy(m, h, peer):
        return pltpu.make_async_remote_copy(
            src_ref=outgoing.at[m, h, peer],
            dst_ref=rows_ref.at[m, h, me],
            send_sem=row_send.at[m, h],
            recv_sem=row_recv.at[m, h],
            device_id={"samp": peer},
            device_id_type=MESH,
        )

    def keep(m, h):
        return pltpu.make_async_copy(outgoing.at[m, h, me], rows_ref.at[m, h, me], own_sem.at[m, h])

    for m, h in parts_of_rows:
        for s in range(samples):
            if h == 0:
                for load in loads(m, s):
                    load.wait()
            jac = lax.dot_general(
                act[s, m], cot[s, m, :, h * 128 : (h + 1) * 128], (((0,), (0,)), ((), ())),
                preferred_element_type=f32,
            )
            wide[pl.ds(h * width * samples + s, width, stride=samples), :] = jac
        for k in range(peers):
            start = h * width * samples + k * share * samples
            block = wide[start : start + share * samples, :]
            outgoing[m, h, k] = block.reshape(share, samples, 128).astype(jnp.bfloat16)
        if (m, h) == (0, 0):
            pl.semaphore_wait(barrier, peers + layers - 2)
            for other in others:
                pl.semaphore_signal(planes, inc=1, device_id={"layer": other}, device_id_type=MESH)
        for peer in steps[::-1] if m == 0 else steps:
            row_copy(m, h, peer).start()
        keep(m, h).start()
    for peer in steps:
        energy_copy(peer).start()
    energy_ref[me] = energy[...]

    for m in range(mats):
        for h in range(halves_of_rows):
            keep(m, h).wait()
            many = rows_ref.at[m, h, 0 : peers - 1]
            pltpu.make_async_copy(many, many, row_recv.at[m, h]).wait()
        left, right = None, None
        for r in range(share):
            rows = whole_rows(rows_ref, m, r)
            halves = rows[: peers * samples // 2], rows[peers * samples // 2 :]
            first = products(rows, halves[0])
            second = products(halves[1], halves[1])
            left, right = (first, second) if r == 0 else (left + first, right + second)
        parts = jnp.concatenate([left, right], axis=0)
        own_gram[...] = parts if m == 0 else own_gram[...] + parts
    pl.semaphore_wait(planes, layers - 1)

    core = me % 2
    device = me * layers + layer

    place = me // 2

    def tile_at(owner_place, plane):
        return pl.ds(pl.multiple_of((owner_place * OWNING + plane) * 8, 8), 8)

    def moved(y, z):
        return (place // 4 + y) % 4 * 4 + (place % 4 + z) % 4

    def owning_core(there, plane):
        return (there * OWNING + plane) % 2

    def piece_copy(there, plane):
        return pltpu.make_async_remote_copy(
            src_ref=own_gram.at[tile_at(there, plane)],
            dst_ref=pieces.at[device],
            send_sem=piece_send,
            recv_sem=piece_recv,
            device_id={"samp": there * 2 + owning_core(there, plane), "layer": plane},
            device_id_type=MESH,
        )

    for y, z in PLACE_STEPS:
        for plane in range(OWNING):
            piece_copy(moved(y, z), plane).start()
    for other in others:

        @pl.when(other < OWNING)
        def _(other=other):
            piece_copy(place, other).start()

    mine = core == owning_core(place, layer)

    @pl.when((layer < OWNING) & jnp.logical_not(mine))
    def _():
        piece_copy(place, layer).start()

    def await_tiles(sem, ref, count):
        many = ref.at[0 : count * 8]
        pltpu.make_async_copy(many, many, sem).wait()

    owns = (layer < OWNING) & mine
    tiles = (peers // 2) * OWNING
    rest = peers * layers - 1

    @pl.when(owns)
    def _():
        pieces[device] = own_gram[tile_at(place, layer)]
        many = pieces.at[0:rest]
        pltpu.make_async_copy(many, many, piece_recv).wait()
        groups = pieces[...].reshape(16, (rest + 1) // 16, 8, 128)
        spread[...] = jnp.sum(jnp.sum(groups, axis=1), axis=0)
        targets = [
            (moved(y, z) * 2 + c, (layer + x) % layers) for y, z, x in CHIP_STEPS for c in range(2)
        ]
        for samp, plane in targets + [(me + 1 - 2 * core, layer)]:
            pltpu.make_async_remote_copy(
                src_ref=spread,
                dst_ref=gram_ref.at[tile_at(place, layer)],
                send_sem=spread_send,
                recv_sem=spread_recv,
                device_id={"samp": samp, "layer": plane},
                device_id_type=MESH,
            ).start()
        gram_ref[tile_at(place, layer)] = spread[...]
        await_tiles(piece_send, own_gram, tiles - 1)
        await_tiles(spread_recv, gram_ref, tiles - 1)
        pltpu.make_async_copy(many, many, spread_send).wait()

    @pl.when(jnp.logical_not(owns))
    def _():
        await_tiles(piece_send, own_gram, tiles)
        await_tiles(spread_recv, gram_ref, tiles)

    for m, h in parts_of_rows:
        many = outgoing.at[m, h, 0 : peers - 1]
        pltpu.make_async_copy(many, many, row_send.at[m, h]).wait()
    many = energy_ref.at[0 : peers - 1]
    pltpu.make_async_copy(many, many, energy_send).wait()
    pltpu.make_async_copy(many, many, energy_recv).wait()


def gram_and_rows(spins, activations, cotangents, offdiag):
    samples, mats, sites, width = activations.shape
    peers, layers = lax.axis_size("samp"), lax.axis_size("layer")
    total, share = peers * samples, width // peers
    bf16 = jnp.bfloat16
    vmem = pl.BlockSpec(memory_space=pltpu.VMEM)
    dma = pltpu.SemaphoreType.DMA
    return pl.pallas_call(
        functools.partial(gram_kernel, peers, layers),
        out_shape=(
            jax.ShapeDtypeStruct((mats, width // 128, peers, share, samples, 128), bf16),
            jax.ShapeDtypeStruct((total // 2 * 3, 128), f32),
            jax.ShapeDtypeStruct((peers, 1, total), f32),
        ),
        in_specs=[pl.BlockSpec(memory_space=pltpu.HBM)] * 4,
        out_specs=(vmem, vmem, vmem),
        scratch_shapes=[
            pltpu.VMEM(spins.shape, jnp.int32),
            pltpu.VMEM((1, samples), f32),
            pltpu.VMEM(activations.shape, bf16),
            pltpu.VMEM(cotangents.shape, bf16),
            pltpu.VMEM((width // 128 * width * samples, 128), f32),
            pltpu.VMEM((mats, width // 128, peers, share, samples, 128), bf16),
            pltpu.VMEM((total // 2 * 3, 128), f32),
            pltpu.VMEM((peers * layers, 8, 128), f32),
            pltpu.VMEM((8, 128), f32),
            pltpu.VMEM((1, total), f32),
            dma((2,)),
            dma,
            dma,
            pltpu.SemaphoreType.REGULAR,
            dma((2, mats, samples)),
            dma((mats, width // 128)),
            dma((mats, width // 128)),
            dma((mats, width // 128)),
            dma,
            dma,
            dma,
            dma,
        ],
        compiler_params=pltpu.CompilerParams(
            collective_id=0, has_side_effects=True, vmem_limit_bytes=20 << 20
        ),
    )(*(pltpu.with_memory_space_constraint(a, pltpu.HBM) for a in (spins, offdiag[None, :], activations, cotangents)))


def eliminate(entry):
    entry = dict(entry)
    inverses, gain = [], {}
    for p in range(0, 8, 2):
        q = p + 1
        first, cross, second = entry[p, p], entry[p, q], entry[q, q]
        scale = 1.0 / (first * second - cross * cross)
        inv = second * scale, cross * scale, first * scale
        inverses.append(inv)
        later = range(p + 2, 8)
        for i in later:
            at_p, at_q = entry[p, i], entry[q, i]
            gain[i, p] = at_p * inv[0] - at_q * inv[1], at_q * inv[2] - at_p * inv[1]
        for i in later:
            for j in range(i, 8):
                entry[i, j] = entry[i, j] - (gain[i, p][0] * entry[p, j] + gain[i, p][1] * entry[q, j])
    return inverses, gain


def forward(gain, values):
    values = list(values)
    for p in range(0, 8, 2):
        for i in range(p + 2, 8):
            by_p, by_q = gain[i, p]
            values[i] = values[i] - (by_p * values[p] + by_q * values[p + 1])
    return values


def scale_pairs(inverses, values):
    scaled = []
    for p in range(0, 8, 2):
        pp, pq, qq = inverses[p // 2]
        first, second = values[p], values[p + 1]
        scaled += [first * pp - second * pq, second * qq - first * pq]
    return scaled


def backward(gain, values):
    values = list(values)
    for p in range(6, -1, -2):
        for i in range(7, p + 1, -1):
            values[p] = values[p] - gain[i, p][0] * values[i]
            values[p + 1] = values[p + 1] - gain[i, p][1] * values[i]
    return values


def tree_sum(terms):
    while len(terms) > 1:
        terms = [a + b for a, b in zip(terms[::2], terms[1::2], strict=True)]
    return terms[0]


def spread_columns(group, start):
    return [jnp.broadcast_to(group[:, start + j : start + j + 1], group.shape) for j in range(8)]


def sweep(groups, k, own_columns, shelf):
    shape = groups[k].shape
    lane, sub = iota(shape, 1), iota(shape, 0)
    start, slot = 8 * k, k % 2

    def put(place, tiles):
        for j, tile in enumerate(tiles):
            shelf[slot, place + 8 * j : place + 8 * j + 8, :] = tile

    def spread_row(place, j, i):
        return shelf[slot, pl.ds(place + 8 * j + i, 8, stride=0), :]

    put(0, own_columns)
    entry = {(i, j): spread_row(0, j, i) for i in range(8) for j in range(i, 8)}
    inverses, gain = eliminate(entry)
    next_columns, columns = None, {}
    if start + 8 < shape[1]:
        near = columns[k + 1] = spread_columns(groups[k + 1], start)
        reduced = forward(gain, near)
        put(64, reduced)
        gains = scale_pairs(inverses, reduced)
        old = spread_columns(groups[k + 1], start + 8)
        next_columns = [
            old[j] - tree_sum([gains[i] * spread_row(64, i, j) for i in range(8)]) for j in range(8)
        ]
    put(128, [groups[k]])
    inside = (lane >= start) & (lane < start + 8)
    marked = [
        jnp.where(inside, jnp.where(lane == start + j, -1.0, 0.0), spread_row(128, 0, j)) for j in range(8)
    ]
    scaled = backward(gain, scale_pairs(inverses, forward(gain, marked)))
    swept = [None] * k
    fresh = scaled[7]
    for i in range(7):
        fresh = jnp.where(sub == i, scaled[i], fresh)
    swept.append(fresh)
    for v in range(k + 1, len(groups)):
        spread = columns.get(v) or spread_columns(groups[v], start)
        swept.append(
            jnp.where(inside, 0.0, groups[v]) - tree_sum([spread[i] * scaled[i] for i in range(8)])
        )
    return swept, next_columns


def solve(matrix, lower, scaled_lower, shelf, rhs):
    half = matrix.shape[0] // 2
    dot = functools.partial(jnp.dot, precision=highest, preferred_element_type=f32)
    count = half // 8
    lane = iota((8, half), 1)
    groups = [matrix[8 * v : 8 * v + 8, 0:half] for v in range(count)]
    groups.append(jnp.broadcast_to(rhs[:, 0:half], (8, half)))
    columns = spread_columns(groups[0], 0)
    for k in range(count):
        pivots = groups[k]
        groups, columns = sweep(groups, k, columns, shelf)
        done, own = lane < 8 * k + 8, lane >= 8 * k
        unit = jnp.where(lane == 8 * k + iota((8, half), 0), -1.0, 0.0)
        lower[8 * k : 8 * k + 8, :] = jnp.where(done, jnp.where(own, unit, pivots), 0.0)
        scaled_lower[8 * k : 8 * k + 8, :] = jnp.where(done, groups[k], 0.0)
    top = groups[count]
    cross = dot(
        lax.dot_general(
            matrix[half : 2 * half, 0:half], lower[...], (((1,), (1,)), ((), ())),
            precision=highest, preferred_element_type=f32,
        ),
        scaled_lower[...],
    )
    rest = matrix[half : 2 * half, half : 2 * half] - dot(cross, matrix[0:half, half : 2 * half])
    groups = [rest[8 * v : 8 * v + 8, :] for v in range(count)]
    groups.append(rhs[:, half : 2 * half] - dot(top, matrix[0:half, half : 2 * half]))
    columns = spread_columns(groups[0], 0)
    for k in range(count):
        groups, columns = sweep(groups, k, columns, shelf)
    bottom = groups[count]
    top = top - dot(bottom, cross)
    return jnp.concatenate([top[0:1, :], bottom[0:1, :]], axis=1)


def solve_kernel(rows_ref, gram_ref, energy_ref, weights_ref, update_ref, work, lower, scaled_lower, shelf):
    mats, halves, peers, share, samples, lanes = rows_ref.shape
    total = peers * samples
    me = lax.axis_index("samp")
    half = total // 2
    corner = gram_ref[half:total, :]
    raw = jnp.concatenate(
        [
            jnp.concatenate([gram_ref[0:half, :], corner.T], axis=1),
            jnp.concatenate([corner, gram_ref[total:, :]], axis=1),
        ],
        axis=0,
    )
    means = jnp.mean(raw, axis=1, keepdims=True)
    diagonal = iota((total, total), 0) == iota((total, total), 1)

    def as_row(col):
        return jnp.sum(jnp.where(diagonal, col, 0.0), axis=0, keepdims=True)

    means_row = as_row(means)
    gram = (raw - means - means_row + jnp.mean(means_row)) / total
    trace = jnp.sum(jnp.where(diagonal, gram, 0.0))
    work[...] = gram + jnp.where(diagonal, SHIFT_RATIO * trace / total, 0.0)
    every = energy_ref[...].reshape(peers, total)
    held = iota((peers, total), 1) // samples == iota((peers, total), 0)
    energy = jnp.sum(jnp.where(held, every, 0.0), axis=0, keepdims=True)
    eps = (energy - jnp.mean(energy)) / jnp.sqrt(f32(total))
    weights = solve(work, lower, scaled_lower, shelf, eps)
    weights_ref[...] = pltpu.roll(weights, total - me * samples, 1)[:, 0:samples]
    coeffs = weights - jnp.mean(weights)
    first = coeffs.astype(jnp.bfloat16)
    rest = coeffs - first.astype(f32)
    second = rest.astype(jnp.bfloat16)
    third = (rest - second.astype(f32)).astype(jnp.bfloat16)
    split = jnp.concatenate(
        [first.astype(f32), second.astype(f32), third.astype(f32), jnp.zeros((5, total), f32)], axis=0
    ).astype(jnp.bfloat16)
    for m in range(mats):
        for r in range(share):
            rows = whole_rows(rows_ref, m, r)
            parts = jnp.dot(split, rows, preferred_element_type=f32)
            update_ref[m, r : r + 1, :] = jnp.sum(parts, axis=0, keepdims=True)


def solve_and_update(rows, gram, energy):
    mats, halves, peers, share, samples, lanes = rows.shape
    width = halves * lanes
    total = peers * samples
    vmem = pl.BlockSpec(memory_space=pltpu.VMEM)
    return pl.pallas_call(
        solve_kernel,
        out_shape=(
            jax.ShapeDtypeStruct((1, samples), f32),
            jax.ShapeDtypeStruct((mats, share, width), f32),
        ),
        in_specs=[vmem, vmem, vmem],
        out_specs=(vmem, vmem),
        scratch_shapes=[
            pltpu.VMEM((total, total), f32),
            pltpu.VMEM((total // 2, total // 2), f32),
            pltpu.VMEM((total // 2, total // 2), f32),
            pltpu.VMEM((2, 136, total // 2), f32),
        ],
        compiler_params=pltpu.CompilerParams(vmem_limit_bytes=20 << 20),
    )(rows, gram, energy)


def body(spins, activations, cotangents, offdiag):
    rows, gram, energy = gram_and_rows(spins, activations, cotangents, offdiag)
    weights, update = solve_and_update(rows, gram, energy)
    return weights[0], update


def solution(mesh):
    placed = (
        P("samp", None),
        P("samp", "layer", None, None),
        P("samp", "layer", None, None),
        P("samp"),
    )
    return jax.shard_map(
        body,
        mesh=mesh,
        in_specs=placed,
        out_specs=(P("samp"), P("layer", "samp", None)),
        check_vma=False,
    )
```
